512 devices in a mesh: seq: 64 (over y, z), tp: 8 (over x, core).
Axes of the slice: x: 4, y: 4, z: 16, core: 2. Of those that a mesh axis runs over, the one named last changes fastest.
Arguments:
- crop_features: bfloat16 [192, 21, 21, 1536], P('seq'), may hold values from -45 to 45
- crop_counts: int32 [64], replicated, may hold values from 1 to 3, as said below
- first_crop: int32 [64], replicated, may hold values from 0 to 127, as said below
- tile_embed: bfloat16 [3, 1536], replicated, may hold values from -3 to 3
- dw_weight: bfloat16 [49, 1536], replicated, may hold values from -0.875 to 0.875
- conv_bias: bfloat16 [1536], replicated, may hold values from -3 to 3
- ln_gain: bfloat16 [1536], replicated, may hold values from 0.099609375 to 1.8984375
- ln_bias: bfloat16 [1536], replicated, may hold values from -2 to 2
- w_up: bfloat16 [1536, 6144], P('seq', 'tp'), may hold values from -0.15625 to 0.15625
- b_up: bfloat16 [6144], P('tp'), may hold values from -3 to 3
- w_down: bfloat16 [6144, 1536], P('tp', 'seq'), may hold values from -0.078125 to 0.078125
- b_down: bfloat16 [1536], P('tp'), may hold values from -2 to 2
- gamma: float32 [1536], P('tp'), may hold values from 0.5 to 2
Outputs:
- visual_rows: bfloat16 [128, 21, 21, 1536], P('seq', None, None, 'tp')
The draws below stay inside these ranges and needn't reach their ends.
Inputs may be any that keep to these rules, and one draw needn't show every extreme that they name: `crop_counts`: the counts sum to 128; 3 is reached in every draw. first_crop[0] is 0 and the entries never fall; device d holds first_crop[d+1] - first_crop[d] crops (the last device 128 - first_crop[last]), at most 3, and some device holds exactly 3; |first_crop[d] - d * 2| <= 1.
All inputs are finite; a program needn't handle non-finite values.
Results may differ from the reference program's by a relative error of at most 0.009.
Values may be sent and summed in bfloat16 or wider, within the bound.
No kernel may reach another device: no remote copies, remote signals or barrier semaphores. Data moves between devices by JAX's collectives and lax.ppermute only.
A program may use at most 128 MiB of HBM per device.

```python
import math
import jax
import jax.numpy as jnp
from jax import lax

C = 1536
FFN = 6144
GRID = 21
KSIZE = 7
MOST_CROPS = 3
CROPS_DEV = 2
SLOTS = 3
CROPS = 128
IMAGES = 64
N_SEQ = 64
N_TP = 8


def draw_crop_features(key, part):
    key_base, key_cols, key_rows = jax.random.split(key, 3)
    full_shape = (N_SEQ * SLOTS, GRID, GRID, C)
    log_low = math.log(0.3)
    log_high = math.log(3.0)
    col_scale = jnp.exp(jax.random.uniform(key_cols, (C,), jnp.float32, log_low, log_high))
    row_scale = jnp.exp(jax.random.uniform(key_rows, (N_SEQ * SLOTS, GRID, GRID, 1), jnp.float32, log_low, log_high))
    base_draw = jax.random.normal(key_base, full_shape, jnp.float32)
    base_draw = jnp.clip(base_draw, -5.0, 5.0)
    return (base_draw * col_scale * row_scale).astype(jnp.bfloat16)


def draw_crop_counts(key, part):
    key_pairs, key_forced, key_value = jax.random.split(key, 3)
    pair_count = IMAGES // 2
    first_of_pair = jax.random.randint(key_pairs, (pair_count,), 1, 4, dtype=jnp.int32)
    forced_pair = jax.random.randint(key_forced, (), 0, pair_count, dtype=jnp.int32)
    forced_value = 1 + 2 * jax.random.randint(key_value, (), 0, 2, dtype=jnp.int32)
    first_of_pair = jnp.where(jnp.arange(pair_count, dtype=jnp.int32) == forced_pair, forced_value, first_of_pair)
    counts = jnp.stack([first_of_pair, 4 - first_of_pair], axis=1).reshape(IMAGES)
    return counts.astype(jnp.int32)


def draw_first_crop(key, part):
    key_walk, key_forced = jax.random.split(jax.random.fold_in(key, 17), 2)
    half_dev = CROPS_DEV // 2
    walk_steps = jax.random.randint(key_walk, (N_SEQ,), -CROPS_DEV, half_dev + 1, dtype=jnp.int32)
    forced_dev = jax.random.randint(key_forced, (), 0, N_SEQ - 1, dtype=jnp.int32)

    def advance(drift_now, inputs):
        dev_id, walk_step = inputs
        drift_next = jnp.clip(drift_now + walk_step, -half_dev, half_dev)
        drift_next = jnp.where(dev_id == 0, 0, drift_next)
        drift_next = jnp.where(dev_id == forced_dev, 0, drift_next)
        drift_next = jnp.where(dev_id == forced_dev + 1, half_dev, drift_next)
        return (drift_next.astype(jnp.int32), drift_next.astype(jnp.int32))
    dev_ids = jnp.arange(N_SEQ, dtype=jnp.int32)
    _, drift = lax.scan(advance, jnp.int32(0), (dev_ids, walk_steps))
    return (dev_ids * CROPS_DEV + drift).astype(jnp.int32)


def levels(own_key, extent, cuts, least, high):
    def one(dim, shards_of):
        heights = jax.random.uniform(jax.random.fold_in(jax.random.fold_in(own_key, 6), dim), (shards_of,), jnp.float32, least / len(cuts), high / len(cuts))
        return jnp.repeat(jnp.exp(heights), extent[dim] // shards_of).reshape((-1,) + (1,) * (len(extent) - dim - 1))

    level = one(*cuts[0])
    for cut in cuts[1:]:
        level = level * one(*cut)
    return level


def scatter_about(own_key, shape, deviation, most, cuts=(), held_as=jnp.bfloat16):
    array = deviation * jax.random.normal(own_key, shape, jnp.float32)
    if cuts:
        array = array * levels(own_key, shape, cuts, -0.22, 0.18)
    return jnp.clip(array, -most, most).astype(held_as)


def setup_inputs(seed: int = 0) -> dict:
    key_of = jax.random.split(jax.random.key(seed), 14)
    return {
        "crop_features": draw_crop_features(jax.random.fold_in(key_of[13], 71), 0),
        "crop_counts": draw_crop_counts(jax.random.fold_in(key_of[13], 71), 0),
        "first_crop": draw_first_crop(jax.random.fold_in(key_of[13], 71), 0),
        "tile_embed": scatter_about(key_of[3], (MOST_CROPS, C), 0.5, 3.0),
        "dw_weight": scatter_about(key_of[4], (KSIZE * KSIZE, C), (KSIZE * KSIZE) ** -0.5, 0.875),
        "conv_bias": scatter_about(key_of[5], (C,), 0.5, 3.0),
        "ln_gain": jnp.clip(1.0 + 0.18 * jax.random.normal(key_of[6], (C,), jnp.float32), 0.099609375, 1.8984375).astype(jnp.bfloat16),
        "ln_bias": scatter_about(key_of[7], (C,), 0.3, 2.0),
        "w_up": scatter_about(key_of[8], (C, FFN), C ** -0.5, 0.15625, ((0, 64), (1, 8))),
        "b_up": scatter_about(key_of[9], (FFN,), 0.5, 3.0, ((0, 8),)),
        "w_down": scatter_about(key_of[10], (FFN, C), FFN ** -0.5, 0.078125, ((0, 8), (1, 64))),
        "b_down": scatter_about(key_of[11], (C,), 0.3, 2.0, ((0, 8),)),
        "gamma": jnp.clip(jnp.exp(math.log(2.0) - 1.3862944 * jax.random.uniform(key_of[12], (C,), jnp.float32) ** levels(key_of[12], (C,), ((0, 8),), -0.2, 0.2)), 0.5, 2.0),
    }


def reference(crop_features, crop_counts, first_crop, tile_embed, dw_weight, conv_bias, ln_gain, ln_bias, w_up, b_up, w_down, b_down, gamma):
    crop_ids = jnp.arange(CROPS, dtype=jnp.int32)
    owners = lax.optimization_barrier(jnp.sum((first_crop[None, :] <= crop_ids[:, None]).astype(jnp.int32), axis=1)) - 1
    slot_rows = (owners * SLOTS + crop_ids - jnp.take(first_crop, owners)).astype(jnp.int32)
    image_start = jnp.cumsum(crop_counts) - crop_counts
    image_begin = lax.optimization_barrier(jnp.max(jnp.where(image_start[None, :] <= crop_ids[:, None], image_start[None, :], 0), axis=1))
    place_ids = (crop_ids - image_begin).astype(jnp.int32)

    def encode_one(inputs):
        slot_row, place_id = inputs
        features = lax.dynamic_index_in_dim(crop_features, slot_row, 0, keepdims=False).astype(jnp.float32)
        tile_row = lax.dynamic_index_in_dim(tile_embed, place_id, 0, keepdims=False).astype(jnp.float32)
        block_in = features + tile_row[None, None, :]
        padded = jnp.pad(block_in, ((3, 3), (3, 3), (0, 0)))
        conv_sum = jnp.zeros_like(block_in)
        for row_shift in range(KSIZE):
            for col_shift in range(KSIZE):
                conv_sum = conv_sum + padded[row_shift:row_shift + GRID, col_shift:col_shift + GRID, :] * dw_weight[row_shift * KSIZE + col_shift].astype(jnp.float32)
        conv_out = (conv_sum + conv_bias.astype(jnp.float32)).reshape(GRID * GRID, C)
        ln_mean = lax.optimization_barrier(jnp.mean(conv_out, axis=1, keepdims=True))
        ln_var = lax.optimization_barrier(jnp.mean((conv_out - ln_mean) ** 2, axis=1, keepdims=True))
        normed = ((conv_out - ln_mean) / jnp.sqrt(ln_var + 1e-06) * ln_gain.astype(jnp.float32) + ln_bias.astype(jnp.float32)).astype(jnp.bfloat16)
        pre_act = jnp.dot(normed, w_up, preferred_element_type=jnp.float32) + b_up.astype(jnp.float32)
        hidden = jax.nn.gelu(pre_act, approximate=False).astype(jnp.bfloat16)
        hidden_groups = hidden.astype(jnp.float32).reshape(GRID * GRID, N_TP, FFN // N_TP)
        weight_groups = w_down.astype(jnp.float32).reshape(N_TP, FFN // N_TP, C)
        partial_value = jnp.einsum('rnh,nhc->nrc', hidden_groups, weight_groups).astype(jnp.bfloat16)
        partial_value = lax.optimization_barrier(partial_value)
        branch = lax.optimization_barrier(jnp.sum(partial_value.astype(jnp.float32), axis=0))
        result = block_in.reshape(GRID * GRID, C) + gamma * (branch + b_down.astype(jnp.float32))
        return result.astype(jnp.bfloat16)
    visual_rows = lax.map(encode_one, (slot_rows, place_ids))
    return visual_rows.reshape(CROPS, GRID, GRID, C)
```

```python
import jax
import jax.numpy as jnp
from jax import lax
from jax.sharding import Mesh, PartitionSpec as P

NY, NZ, NX, NCORE = 4, 16, 4, 2
SEQ = ("y", "z")
TP = ("x", "core")
PER_DEV = 2
KSIDE = 7


def shift(block, axis, distance, size):
    return lax.ppermute(block, axis, [(i, (i + distance) % size) for i in range(size)])


def gather_weights(w_up, w_down):
    both = jnp.stack([w_up, w_down.T])
    over_y = lax.all_gather(both, "y", axis=1)
    over_z = lax.all_gather(over_y, "z", axis=2)
    return over_z.reshape(2, NY * NZ * w_up.shape[0], w_up.shape[1])


def regroup(slots, seq_index, first_crop):
    count = NY * NZ
    first = first_crop[seq_index]
    limit = jnp.where(
        seq_index + 1 < count, first_crop[jnp.minimum(seq_index + 1, count - 1)], PER_DEV * count
    )
    last_slot = slots.shape[0] - 1

    def crop(number):
        return lax.dynamic_index_in_dim(
            slots, jnp.clip(number - first, 0, last_slot), 0, keepdims=False
        )

    target = PER_DEV * seq_index
    up = lax.ppermute(
        crop(target + PER_DEV), SEQ, [(i, i + 1) for i in range(count - 1)]
    )
    down = lax.ppermute(crop(target - 1), SEQ, [(i + 1, i) for i in range(count - 1)])
    crop_a = jnp.where(first <= target, crop(target), up)
    crop_b = jnp.where(limit > target + 1, crop(target + 1), down)
    return jnp.stack([crop_a, crop_b])


def depthwise(block_in, weight, bias):
    side = block_in.shape[1]
    padded = jnp.pad(block_in, ((0, 0), (3, 3), (3, 3), (0, 0)))
    total = jnp.zeros_like(block_in)
    for a in range(KSIDE):
        for b in range(KSIDE):
            total = total + padded[:, a : a + side, b : b + side, :] * weight[a * KSIDE + b]
    return total + bias


def scatter_sum(partial, width):
    core = lax.axis_index("core")
    x = lax.axis_index("x")
    parts = partial.reshape(NX, NCORE, width, partial.shape[1])
    mine = lax.dynamic_index_in_dim(parts, core, 1, keepdims=False)
    other = lax.dynamic_index_in_dim(parts, 1 - core, 1, keepdims=False)
    other = shift(other, "core", 1, NCORE)
    pair = (mine.astype(jnp.float32) + other.astype(jnp.float32)).astype(jnp.bfloat16)

    def part(distance):
        return lax.dynamic_index_in_dim(pair, lax.rem(x + distance, NX), 0, keepdims=False)

    total = part(0).astype(jnp.float32)
    for distance in (2, 1, 3):
        total = total + shift(part(distance), "x", distance, NX).astype(jnp.float32)
    return total


def per_device(
    crop_features, crop_counts, first_crop, tile_embed, dw_weight, conv_bias,
    ln_gain, ln_bias, w_up, b_up, w_down, b_down, gamma,
):
    f32 = jnp.float32
    width = b_down.shape[0]
    side = crop_features.shape[1]
    seq_index = lax.axis_index(SEQ)
    start = lax.axis_index(TP) * width
    weights = gather_weights(w_up, w_down)

    def channels(array):
        return lax.dynamic_slice_in_dim(array, start, width, array.ndim - 1)

    crops = regroup(channels(crop_features), seq_index, first_crop)
    crop_ids = PER_DEV * seq_index + jnp.arange(PER_DEV, dtype=jnp.int32)
    image_start = jnp.cumsum(crop_counts) - crop_counts
    begin = jnp.max(
        jnp.where(image_start[None, :] <= crop_ids[:, None], image_start[None, :], 0), axis=1
    )
    choose = (crop_ids - begin)[:, None] == jnp.arange(tile_embed.shape[0])[None, :]
    tile = jnp.sum(
        jnp.where(choose[:, :, None], channels(tile_embed).astype(f32)[None], 0.0), axis=1
    )
    block_in = crops.astype(f32) + tile[:, None, None, :]
    conv = depthwise(block_in, channels(dw_weight).astype(f32), channels(conv_bias).astype(f32))
    cells = PER_DEV * side * side
    conv_t = conv.reshape(cells, width).T.astype(jnp.float16)
    conv_all = lax.all_gather(conv_t, TP, axis=0, tiled=True).astype(f32)
    mean = jnp.mean(conv_all, axis=0, keepdims=True)
    var = jnp.mean((conv_all - mean) ** 2, axis=0, keepdims=True)
    normed = (
        (conv_all - mean) / jnp.sqrt(var + 1e-6) * ln_gain.astype(f32)[:, None]
        + ln_bias.astype(f32)[:, None]
    ).astype(jnp.bfloat16)
    pre_act = lax.dot_general(
        weights[0], normed, (((0,), (0,)), ((), ())), preferred_element_type=f32
    )
    hidden = jax.nn.gelu(pre_act + b_up.astype(f32)[:, None], approximate=False).astype(jnp.bfloat16)
    partial = jnp.dot(weights[1], hidden, preferred_element_type=f32).astype(jnp.bfloat16)
    branch = scatter_sum(partial, width)
    scaled = (gamma[:, None] * (branch + b_down.astype(f32)[:, None])).T
    result = block_in.reshape(cells, width) + scaled
    return result.astype(jnp.bfloat16).reshape(PER_DEV, side, side, width)


def solution(mesh):
    fine = Mesh(mesh.devices.reshape(NY, NZ, NX, NCORE), SEQ + TP)
    placed = (
        P(SEQ, None, None, None), P(), P(), P(), P(), P(), P(), P(),
        P(SEQ, TP), P(TP), P(TP, SEQ), P(TP), P(TP),
    )
    return jax.shard_map(
        per_device,
        mesh=fine,
        in_specs=placed,
        out_specs=P(SEQ, None, None, TP),
        check_vma=False,
    )
```

```python
import jax
import jax.numpy as jnp
from jax import lax
from jax.experimental import pallas as pl
from jax.experimental.pallas import tpu as pltpu
from jax.sharding import Mesh, PartitionSpec as P

NY, NZ, NX, NCORE = 4, 16, 4, 2
SEQ = ("y", "z")
TP = ("x", "core")
PER_DEV = 2
KSIDE = 7


def shift(block, axis, distance, size):
    return lax.ppermute(block, axis, [(i, (i + distance) % size) for i in range(size)])


def gather_weights(w_up, w_down):
    both = jnp.stack([w_up, w_down.T])
    over_y = lax.all_gather(both, "y", axis=1)
    over_z = lax.all_gather(over_y, "z", axis=2)
    return over_z.reshape(2, NY * NZ * w_up.shape[0], w_up.shape[1])


def regroup(slots, seq_index, first_crop):
    count = NY * NZ
    first = first_crop[seq_index]
    limit = jnp.where(
        seq_index + 1 < count, first_crop[jnp.minimum(seq_index + 1, count - 1)], PER_DEV * count
    )
    last_slot = slots.shape[0] - 1

    def crop(number):
        return lax.dynamic_index_in_dim(
            slots, jnp.clip(number - first, 0, last_slot), 0, keepdims=False
        )

    target = PER_DEV * seq_index
    up = lax.ppermute(
        crop(target + PER_DEV), SEQ, [(i, i + 1) for i in range(count - 1)]
    )
    down = lax.ppermute(crop(target - 1), SEQ, [(i + 1, i) for i in range(count - 1)])
    crop_a = jnp.where(first <= target, crop(target), up)
    crop_b = jnp.where(limit > target + 1, crop(target + 1), down)
    return jnp.stack([crop_a, crop_b])


def depthwise(block_in, weight, bias):
    side = block_in.shape[1]
    padded = jnp.pad(block_in, ((0, 0), (3, 3), (3, 3), (0, 0)))
    total = jnp.zeros_like(block_in)
    for a in range(KSIDE):
        for b in range(KSIDE):
            total = total + padded[:, a : a + side, b : b + side, :] * weight[a * KSIDE + b]
    return total + bias


def whole(space=pltpu.VMEM):
    return pl.BlockSpec(memory_space=space)


def copy_down_rows(weights, buffer, sems, core):
    width = buffer.shape[0] // NX
    copies = []
    for x in range(NX):
        row = pl.multiple_of((x * NCORE + core) * width, width)
        copies.append(
            pltpu.make_async_copy(
                weights.at[1, pl.ds(row, width), :],
                buffer.at[pl.ds(x * width, width), :],
                sems.at[x],
            )
        )
    return copies


def down_product(buffer, hidden, out):
    width = buffer.shape[0] // NX
    product = lax.dot_general(
        buffer[...], hidden, (((1,), (1,)), ((), ())), preferred_element_type=jnp.float32
    )
    for x in range(NX):
        out[x] = product[x * width : (x + 1) * width].astype(out.dtype)


def first_kernel(core, normed, b_up, weights, hidden, out, up, down, up_sem, down_sem):
    units = up.shape[1]
    pieces = up_sem.shape[0]
    step = units // pieces
    ups = []
    for p in range(pieces):
        span = pl.ds(p * step, step)
        ups.append(
            pltpu.make_async_copy(weights.at[0, :, span], up.at[:, span], up_sem.at[p])
        )
    for copy in ups:
        copy.start()
    downs = copy_down_rows(weights, down, down_sem, 1 - core[0])
    for copy in downs:
        copy.start()
    for p in range(pieces):
        span = pl.ds(p * step, step)
        ups[p].wait()
        pre = jnp.dot(normed[...], up[:, span], preferred_element_type=jnp.float32)
        pre = pre + b_up[:, span]
        act = 0.5 * pre * (1.0 + lax.erf(pre * 0.5**0.5))
        hidden[:, span] = act.astype(hidden.dtype)
    for copy in downs:
        copy.wait()
    down_product(down, hidden[...], out)


def second_kernel(core, hidden, weights, out, down, down_sem):
    downs = copy_down_rows(weights, down, down_sem, core[0])
    for copy in downs:
        copy.start()
    for copy in downs:
        copy.wait()
    down_product(down, hidden[...], out)


def pair_kernel(x, mine, other, own, ahead, behind, far_a, far_b):
    def pair(distance):
        i = lax.rem(x[0] + distance, NX)
        return mine[i].astype(jnp.float32) + other[i].astype(jnp.float32)

    half = far_a.shape[0]
    own[...] = pair(0)
    ahead[...] = pair(1).astype(ahead.dtype)
    behind[...] = pair(3).astype(behind.dtype)
    far = pair(2)
    far_a[...] = far[:half].astype(far_a.dtype)
    far_b[...] = far[half:].astype(far_b.dtype)


def last_kernel(own, ahead, behind, b_down, gamma, residual, out):
    total = own[...] + ahead[...].astype(jnp.float32) + behind[...].astype(jnp.float32)
    scaled = gamma[...] * (total + b_down[...])
    rows = residual.shape[0]
    out[...] = (residual[...] + scaled.T[:rows]).astype(out.dtype)


def mlp_sum(normed, weights, b_up, width):
    bf16, f32 = jnp.bfloat16, jnp.float32
    cells, units = normed.shape[0], b_up.shape[0]
    core = lax.axis_index("core").astype(jnp.int32).reshape(1)
    x = lax.axis_index("x").astype(jnp.int32).reshape(1)
    params = pltpu.CompilerParams(vmem_limit_bytes=48 * 2**20)
    half_out = jax.ShapeDtypeStruct((NX, width, cells), bf16)
    down = pltpu.VMEM((NX * width, units), bf16)
    hidden, other = pl.pallas_call(
        first_kernel,
        out_shape=(jax.ShapeDtypeStruct((cells, units), bf16), half_out),
        in_specs=[whole(pltpu.SMEM), whole(), whole(), whole(pl.ANY)],
        out_specs=(whole(), whole()),
        scratch_shapes=[
            pltpu.VMEM(weights.shape[1:], bf16),
            down,
            pltpu.SemaphoreType.DMA((3,)),
            pltpu.SemaphoreType.DMA((NX,)),
        ],
        compiler_params=params,
        name="up_and_down",
    )(core, normed, b_up.astype(f32)[None, :], weights)
    other = shift(other, "core", 1, NCORE)
    mine = pl.pallas_call(
        second_kernel,
        out_shape=half_out,
        in_specs=[whole(pltpu.SMEM), whole(), whole(pl.ANY)],
        out_specs=whole(),
        scratch_shapes=[down, pltpu.SemaphoreType.DMA((NX,))],
        compiler_params=params,
        name="down_own",
    )(core, hidden, weights)
    full = jax.ShapeDtypeStruct((width, cells), bf16)
    half = jax.ShapeDtypeStruct((width // 2, cells), bf16)
    own, ahead, behind, far_a, far_b = pl.pallas_call(
        pair_kernel,
        out_shape=(jax.ShapeDtypeStruct((width, cells), f32), full, full, half, half),
        in_specs=[whole(pltpu.SMEM), whole(), whole()],
        out_specs=(whole(),) * 5,
        compiler_params=params,
        name="pair",
    )(x, mine, other)
    far_a = shift(far_a, "x", 1, NX)
    far_b = shift(far_b, "x", -1, NX)
    ahead = jnp.concatenate([ahead[: width // 2] + far_a, ahead[width // 2 :]])
    behind = jnp.concatenate([behind[: width // 2], behind[width // 2 :] + far_b])
    return own, shift(ahead, "x", 1, NX), shift(behind, "x", -1, NX)


def per_device(
    crop_features, crop_counts, first_crop, tile_embed, dw_weight, conv_bias,
    ln_gain, ln_bias, w_up, b_up, w_down, b_down, gamma,
):
    f32 = jnp.float32
    width = b_down.shape[0]
    side = crop_features.shape[1]
    seq_index = lax.axis_index(SEQ)
    start = lax.axis_index(TP) * width
    weights = gather_weights(w_up, w_down)

    def channels(array):
        return lax.dynamic_slice_in_dim(array, start, width, array.ndim - 1)

    crops = regroup(channels(crop_features), seq_index, first_crop)
    crop_ids = PER_DEV * seq_index + jnp.arange(PER_DEV, dtype=jnp.int32)
    image_start = jnp.cumsum(crop_counts) - crop_counts
    begin = jnp.max(
        jnp.where(image_start[None, :] <= crop_ids[:, None], image_start[None, :], 0), axis=1
    )
    choose = (crop_ids - begin)[:, None] == jnp.arange(tile_embed.shape[0])[None, :]
    tile = jnp.sum(
        jnp.where(choose[:, :, None], channels(tile_embed).astype(f32)[None], 0.0), axis=1
    )
    block_in = crops.astype(f32) + tile[:, None, None, :]
    conv = depthwise(block_in, channels(dw_weight).astype(f32), channels(conv_bias).astype(f32))
    cells = PER_DEV * side * side
    padding = -cells % 128
    conv_t = jnp.pad(conv.reshape(cells, width), ((0, padding), (0, 0))).T.astype(jnp.float16)
    conv_all = lax.all_gather(conv_t, TP, axis=0, tiled=True).astype(f32)
    mean = jnp.mean(conv_all, axis=0, keepdims=True)
    var = jnp.mean((conv_all - mean) ** 2, axis=0, keepdims=True)
    normed = (
        (conv_all - mean) / jnp.sqrt(var + 1e-6) * ln_gain.astype(f32)[:, None]
        + ln_bias.astype(f32)[:, None]
    ).astype(jnp.bfloat16).T
    own, ahead, behind = mlp_sum(normed, weights, b_up, width)
    result = pl.pallas_call(
        last_kernel,
        out_shape=jax.ShapeDtypeStruct((cells, width), jnp.bfloat16),
        in_specs=[whole()] * 6,
        out_specs=whole(),
        compiler_params=pltpu.CompilerParams(vmem_limit_bytes=48 * 2**20),
        name="result",
    )(own, ahead, behind, b_down.astype(f32)[:, None], gamma[:, None], block_in.reshape(cells, width))
    return result.reshape(PER_DEV, side, side, width)


def solution(mesh):
    fine = Mesh(mesh.devices.reshape(NY, NZ, NX, NCORE), SEQ + TP)
    placed = (
        P(SEQ, None, None, None), P(), P(), P(), P(), P(), P(), P(),
        P(SEQ, TP), P(TP), P(TP, SEQ), P(TP), P(TP),
    )
    return jax.shard_map(
        per_device,
        mesh=fine,
        in_specs=placed,
        out_specs=P(SEQ, None, None, TP),
        check_vma=False,
    )
```

```python
import jax
import jax.numpy as jnp
from jax import lax
from jax.experimental import pallas as pl
from jax.experimental.pallas import tpu as pltpu
from jax.sharding import Mesh, PartitionSpec as P

NY, NZ, NX, NCORE = 4, 16, 4, 2
SEQ = ("y", "z")
TP = ("x", "core")
PER_DEV = 2
KSIDE = 7
DISTANCES = (2, 1, 3)


def shift(block, axis, distance, size):
    return lax.ppermute(block, axis, [(i, (i + distance) % size) for i in range(size)])


def gather_weights(w_up, w_down):
    both = jnp.stack([w_up, w_down.T])
    over_y = lax.all_gather(both, "y", axis=1)
    over_z = lax.all_gather(over_y, "z", axis=2)
    return over_z.reshape(2, NY * NZ * w_up.shape[0], w_up.shape[1])


def regroup(slots, seq_index, first_crop):
    count = NY * NZ
    first = first_crop[seq_index]
    limit = jnp.where(
        seq_index + 1 < count, first_crop[jnp.minimum(seq_index + 1, count - 1)], PER_DEV * count
    )
    last_slot = slots.shape[0] - 1

    def crop(number):
        return lax.dynamic_index_in_dim(
            slots, jnp.clip(number - first, 0, last_slot), 0, keepdims=False
        )

    target = PER_DEV * seq_index
    up = lax.ppermute(
        crop(target + PER_DEV), SEQ, [(i, i + 1) for i in range(count - 1)]
    )
    down = lax.ppermute(crop(target - 1), SEQ, [(i + 1, i) for i in range(count - 1)])
    crop_a = jnp.where(first <= target, crop(target), up)
    crop_b = jnp.where(limit > target + 1, crop(target + 1), down)
    return jnp.stack([crop_a, crop_b])


def depthwise(block_in, weight, bias):
    side = block_in.shape[1]
    padded = jnp.pad(block_in, ((0, 0), (3, 3), (3, 3), (0, 0)))
    total = jnp.zeros_like(block_in)
    for a in range(KSIDE):
        for b in range(KSIDE):
            total = total + padded[:, a : a + side, b : b + side, :] * weight[a * KSIDE + b]
    return total + bias


def whole(space=pltpu.VMEM):
    return pl.BlockSpec(memory_space=space)


def copy_down_rows(weights, buffer, sems, core):
    width = buffer.shape[0] // NX
    copies = []
    for x in range(NX):
        row = pl.multiple_of((x * NCORE + core) * width, width)
        copies.append(
            pltpu.make_async_copy(
                weights.at[1, pl.ds(row, width), :],
                buffer.at[pl.ds(x * width, width), :],
                sems.at[x],
            )
        )
    return copies


def down_product(buffer, hidden, out):
    width = buffer.shape[0] // NX
    product = lax.dot_general(
        buffer[...], hidden, (((1,), (1,)), ((), ())), preferred_element_type=jnp.float32
    )
    for x in range(NX):
        out[x] = product[x * width : (x + 1) * width].astype(out.dtype)


def first_kernel(core, normed, b_up, weights, hidden, out, up, down, up_sem, down_sem):
    ups = []
    pieces = up_sem.shape[0]
    step = up.shape[0] // pieces
    for p in range(pieces):
        span = pl.ds(p * step, step)
        ups.append(pltpu.make_async_copy(weights.at[0, span, :], up.at[span, :], up_sem.at[p]))
    for copy in ups:
        copy.start()
    downs = copy_down_rows(weights, down, down_sem, 1 - core[0])
    for copy in downs:
        copy.start()
    for copy in ups:
        copy.wait()
    cells = normed.shape[0]
    rows = cells // 4
    for r in range(0, cells, rows):
        pre = jnp.dot(normed[r : r + rows], up[...], preferred_element_type=jnp.float32)
        pre = pre + b_up[...]
        act = 0.5 * pre * (1.0 + lax.erf(pre * 0.5**0.5))
        hidden[r : r + rows] = act.astype(hidden.dtype)
    for copy in downs:
        copy.wait()
    down_product(down, hidden[...], out)


def second_kernel(core, hidden, weights, out, down, down_sem):
    downs = copy_down_rows(weights, down, down_sem, core[0])
    for copy in downs:
        copy.start()
    for copy in downs:
        copy.wait()
    down_product(down, hidden[...], out)


def pair_kernel(x, mine, other, own, *sent):
    def pair(distance):
        i = lax.rem(x[0] + distance, NX)
        return mine[i].astype(jnp.float32) + other[i].astype(jnp.float32)

    own[...] = pair(0)
    for distance, block in zip(DISTANCES, sent):
        block[...] = pair(distance).astype(block.dtype)


def last_kernel(own, first, second, third, b_down, gamma, residual, out):
    total = own[...]
    for block in (first, second, third):
        total = total + block[...].astype(jnp.float32)
    scaled = gamma[...] * (total + b_down[...])
    rows = residual.shape[0]
    out[...] = (residual[...] + scaled.T[:rows]).astype(out.dtype)


def mlp_sum(normed, weights, b_up, width):
    bf16, f32 = jnp.bfloat16, jnp.float32
    cells, units = normed.shape[0], b_up.shape[0]
    core = lax.axis_index("core").astype(jnp.int32).reshape(1)
    x = lax.axis_index("x").astype(jnp.int32).reshape(1)
    params = pltpu.CompilerParams(vmem_limit_bytes=48 * 2**20)
    half_out = jax.ShapeDtypeStruct((NX, width, cells), bf16)
    down = pltpu.VMEM((NX * width, units), bf16)
    hidden, other = pl.pallas_call(
        first_kernel,
        out_shape=(jax.ShapeDtypeStruct((cells, units), bf16), half_out),
        in_specs=[whole(pltpu.SMEM), whole(), whole(), whole(pl.ANY)],
        out_specs=(whole(), whole()),
        scratch_shapes=[
            pltpu.VMEM(weights.shape[1:], bf16),
            down,
            pltpu.SemaphoreType.DMA((4,)),
            pltpu.SemaphoreType.DMA((NX,)),
        ],
        compiler_params=params,
        name="up_and_down",
    )(core, normed, b_up.astype(f32)[None, :], weights)
    other = shift(other, "core", 1, NCORE)
    mine = pl.pallas_call(
        second_kernel,
        out_shape=half_out,
        in_specs=[whole(pltpu.SMEM), whole(), whole(pl.ANY)],
        out_specs=whole(),
        scratch_shapes=[down, pltpu.SemaphoreType.DMA((NX,))],
        compiler_params=params,
        name="down_own",
    )(core, hidden, weights)
    block = jax.ShapeDtypeStruct((width, cells), bf16)
    own, *sent = pl.pallas_call(
        pair_kernel,
        out_shape=(jax.ShapeDtypeStruct((width, cells), f32),) + (block,) * len(DISTANCES),
        in_specs=[whole(pltpu.SMEM), whole(), whole()],
        out_specs=(whole(),) * (1 + len(DISTANCES)),
        compiler_params=params,
        name="pair",
    )(x, mine, other)
    return own, *(shift(block, "x", d, NX) for d, block in zip(DISTANCES, sent))


def per_device(
    crop_features, crop_counts, first_crop, tile_embed, dw_weight, conv_bias,
    ln_gain, ln_bias, w_up, b_up, w_down, b_down, gamma,
):
    f32 = jnp.float32
    width = b_down.shape[0]
    side = crop_features.shape[1]
    seq_index = lax.axis_index(SEQ)
    start = lax.axis_index(TP) * width
    weights = gather_weights(w_up, w_down)

    def channels(array):
        return lax.dynamic_slice_in_dim(array, start, width, array.ndim - 1)

    crops = regroup(channels(crop_features), seq_index, first_crop)
    crop_ids = PER_DEV * seq_index + jnp.arange(PER_DEV, dtype=jnp.int32)
    image_start = jnp.cumsum(crop_counts) - crop_counts
    begin = jnp.max(
        jnp.where(image_start[None, :] <= crop_ids[:, None], image_start[None, :], 0), axis=1
    )
    choose = (crop_ids - begin)[:, None] == jnp.arange(tile_embed.shape[0])[None, :]
    tile = jnp.sum(
        jnp.where(choose[:, :, None], channels(tile_embed).astype(f32)[None], 0.0), axis=1
    )
    block_in = crops.astype(f32) + tile[:, None, None, :]
    conv = depthwise(block_in, channels(dw_weight).astype(f32), channels(conv_bias).astype(f32))
    cells = PER_DEV * side * side
    padding = -cells % 128
    conv_t = jnp.pad(conv.reshape(cells, width), ((0, padding), (0, 0))).T.astype(jnp.float16)
    conv_all = lax.all_gather(conv_t, TP, axis=0, tiled=True).astype(f32)
    mean = jnp.mean(conv_all, axis=0, keepdims=True)
    var = jnp.mean((conv_all - mean) ** 2, axis=0, keepdims=True)
    normed = (
        (conv_all - mean) / jnp.sqrt(var + 1e-6) * ln_gain.astype(f32)[:, None]
        + ln_bias.astype(f32)[:, None]
    ).astype(jnp.bfloat16).T
    sums = mlp_sum(normed, weights, b_up, width)
    result = pl.pallas_call(
        last_kernel,
        out_shape=jax.ShapeDtypeStruct((cells, width), jnp.bfloat16),
        in_specs=[whole()] * (len(sums) + 3),
        out_specs=whole(),
        compiler_params=pltpu.CompilerParams(vmem_limit_bytes=48 * 2**20),
        name="result",
    )(*sums, b_down.astype(f32)[:, None], gamma[:, None], block_in.reshape(cells, width))
    return result.reshape(PER_DEV, side, side, width)


def solution(mesh):
    fine = Mesh(mesh.devices.reshape(NY, NZ, NX, NCORE), SEQ + TP)
    placed = (
        P(SEQ, None, None, None), P(), P(), P(), P(), P(), P(), P(),
        P(SEQ, TP), P(TP), P(TP, SEQ), P(TP), P(TP),
    )
    return jax.shard_map(
        per_device,
        mesh=fine,
        in_specs=placed,
        out_specs=P(SEQ, None, None, TP),
        check_vma=False,
    )
```

```python
import jax
import jax.numpy as jnp
from jax import lax
from jax.experimental import pallas as pl
from jax.experimental.pallas import tpu as pltpu
from jax.sharding import Mesh, PartitionSpec as P

NY, NZ, NX, NCORE = 4, 16, 4, 2
SEQ = ("y", "z")
TP = ("x", "core")
PER_DEV = 2
KSIDE = 7
DISTANCES = (2, 1, 3)


def shift(block, axis, distance, size):
    return lax.ppermute(block, axis, [(i, (i + distance) % size) for i in range(size)])


def gather_weights(w_up, w_down):
    both = jnp.stack([w_up, w_down.T])
    over_y = lax.all_gather(both, "y", axis=1)
    over_z = lax.all_gather(over_y, "z", axis=2)
    return over_z.reshape(2, NY * NZ * w_up.shape[0], w_up.shape[1])


def exchange(slots, seq_index, first_crop):
    count = NY * NZ
    first = first_crop[seq_index]
    last_slot = slots.shape[0] - 1

    def crop(number):
        return lax.dynamic_index_in_dim(
            slots, jnp.clip(number - first, 0, last_slot), 0, keepdims=False
        )

    target = PER_DEV * seq_index
    before = lax.ppermute(
        crop(target + PER_DEV), SEQ, [(i, i + 1) for i in range(count - 1)]
    )
    after = lax.ppermute(crop(target - 1), SEQ, [(i + 1, i) for i in range(count - 1)])
    return before, after


def conv_kernel(
    seq, first_crop, crop_counts, slots, before, after, table, block_in, conv, padded, shifted, taps
):
    f32 = jnp.float32
    side = block_in.shape[1]
    shards = first_crop.shape[0]
    margin = KSIDE // 2
    here = seq[0]
    first = first_crop[here]
    limit = jnp.where(
        here + 1 < shards, first_crop[jnp.minimum(here + 1, shards - 1)], PER_DEV * shards
    )
    tile_at = KSIDE * KSIDE
    bias = table[tile_at + 3 : tile_at + 4, :].astype(f32)
    for t in range(KSIDE * KSIDE):
        taps[t] = jnp.broadcast_to(table[t : t + 1, :].astype(f32), taps.shape[1:])
    padded[...] = jnp.zeros_like(padded)
    shifted[...] = jnp.zeros_like(shifted)
    for n in range(PER_DEV):
        target = PER_DEV * here + n

        def image(i, carry):
            start, begin = carry
            return start + crop_counts[i], jnp.where(start <= target, start, begin)

        _, begin = lax.fori_loop(0, crop_counts.shape[0], image, (jnp.int32(0), jnp.int32(0)))
        place = target - begin
        tile = jnp.zeros_like(bias)
        for p in range(3):
            row = table[tile_at + p : tile_at + p + 1, :].astype(f32)
            tile = jnp.where(place == p, row, tile)
        mine = slots[jnp.clip(target - first, 0, slots.shape[0] - 1)].astype(f32)
        received = (before if n == 0 else after)[...].astype(f32)
        held = (first <= target) & (target < limit)
        crop = jnp.where(held, mine, received) + tile
        block_in[n] = crop
        padded[:, margin : margin + side, :] = crop
        for b in range(KSIDE):
            shifted[b, n, margin : margin + side] = padded[:, b : b + shifted.shape[3], :]
    columns, width = shifted.shape[3:]
    groups = side // 3

    def three_rows(g, _):
        n, top = lax.div(g, groups), lax.rem(g, groups) * 3
        sums = [jnp.zeros((columns // 8, 8, width), f32) for _ in range(3)]
        for b in range(KSIDE):
            for r in range(KSIDE + 2):
                row = shifted[b, n, top + r].reshape(columns // 8, 8, width)
                for o in range(3):
                    if 0 <= r - o < KSIDE:
                        sums[o] = sums[o] + row * taps[(r - o) * KSIDE + b][None]
        for o in range(3):
            conv[n, top + o] = sums[o].reshape(columns, width) + bias
        return 0

    lax.fori_loop(0, PER_DEV * groups, three_rows, 0)


def depthwise(seq_index, first_crop, crop_counts, slots, before, after, table):
    f32 = jnp.float32
    side, width = slots.shape[1], slots.shape[3]
    columns = 24
    return pl.pallas_call(
        conv_kernel,
        out_shape=(
            jax.ShapeDtypeStruct((PER_DEV, side, side, width), f32),
            jax.ShapeDtypeStruct((PER_DEV, side, columns, width), f32),
        ),
        in_specs=[whole(pltpu.SMEM)] * 3 + [whole()] * 4,
        out_specs=(whole(), whole()),
        scratch_shapes=[
            pltpu.VMEM((side, columns + 8, width), f32),
            pltpu.VMEM((KSIDE, PER_DEV, side + 6, columns, width), f32),
            pltpu.VMEM((KSIDE * KSIDE, 8, width), f32),
        ],
        compiler_params=pltpu.CompilerParams(vmem_limit_bytes=48 * 2**20),
        name="conv",
    )(seq_index.astype(jnp.int32).reshape(1), first_crop, crop_counts, slots, before, after, table)


def whole(space=pltpu.VMEM):
    return pl.BlockSpec(memory_space=space)


def copy_down_rows(weights, buffer, sems, core):
    width = buffer.shape[0] // NX
    copies = []
    for x in range(NX):
        row = pl.multiple_of((x * NCORE + core) * width, width)
        copies.append(
            pltpu.make_async_copy(
                weights.at[1, pl.ds(row, width), :],
                buffer.at[pl.ds(x * width, width), :],
                sems.at[x],
            )
        )
    return copies


def down_product(buffer, hidden, out):
    width = buffer.shape[0] // NX
    product = lax.dot_general(
        buffer[...], hidden, (((1,), (1,)), ((), ())), preferred_element_type=jnp.float32
    )
    for x in range(NX):
        out[x] = product[x * width : (x + 1) * width].astype(out.dtype)


def first_kernel(core, normed, b_up, weights, hidden, out, up, down, up_sem, down_sem):
    ups = []
    pieces = up_sem.shape[0]
    step = up.shape[0] // pieces
    for p in range(pieces):
        span = pl.ds(p * step, step)
        ups.append(pltpu.make_async_copy(weights.at[0, span, :], up.at[span, :], up_sem.at[p]))
    for copy in ups:
        copy.start()
    downs = copy_down_rows(weights, down, down_sem, 1 - core[0])
    for copy in downs:
        copy.start()
    for copy in ups:
        copy.wait()
    cells = normed.shape[0]
    rows = cells // 4
    for r in range(0, cells, rows):
        pre = jnp.dot(normed[r : r + rows], up[...], preferred_element_type=jnp.float32)
        pre = pre + b_up[...]
        act = 0.5 * pre * (1.0 + lax.erf(pre * 0.5**0.5))
        hidden[r : r + rows] = act.astype(hidden.dtype)
    for copy in downs:
        copy.wait()
    down_product(down, hidden[...], out)


def second_kernel(core, hidden, weights, out, down, down_sem):
    downs = copy_down_rows(weights, down, down_sem, core[0])
    for copy in downs:
        copy.start()
    for copy in downs:
        copy.wait()
    down_product(down, hidden[...], out)


def pair_kernel(x, mine, other, own, *sent):
    def pair(distance):
        i = lax.rem(x[0] + distance, NX)
        return mine[i].astype(jnp.float32) + other[i].astype(jnp.float32)

    own[...] = pair(0)
    for distance, block in zip(DISTANCES, sent):
        block[...] = pair(distance).astype(block.dtype)


def last_kernel(own, first, second, third, b_down, gamma, residual, out):
    total = own[...]
    for block in (first, second, third):
        total = total + block[...].astype(jnp.float32)
    scaled = gamma[...] * (total + b_down[...])
    rows = residual.shape[0]
    out[...] = (residual[...] + scaled.T[:rows]).astype(out.dtype)


def mlp_sum(normed, weights, b_up, width):
    bf16, f32 = jnp.bfloat16, jnp.float32
    cells, units = normed.shape[0], b_up.shape[0]
    core = lax.axis_index("core").astype(jnp.int32).reshape(1)
    x = lax.axis_index("x").astype(jnp.int32).reshape(1)
    params = pltpu.CompilerParams(vmem_limit_bytes=48 * 2**20)
    half_out = jax.ShapeDtypeStruct((NX, width, cells), bf16)
    down = pltpu.VMEM((NX * width, units), bf16)
    hidden, other = pl.pallas_call(
        first_kernel,
        out_shape=(jax.ShapeDtypeStruct((cells, units), bf16), half_out),
        in_specs=[whole(pltpu.SMEM), whole(), whole(), whole(pl.ANY)],
        out_specs=(whole(), whole()),
        scratch_shapes=[
            pltpu.VMEM(weights.shape[1:], bf16),
            down,
            pltpu.SemaphoreType.DMA((4,)),
            pltpu.SemaphoreType.DMA((NX,)),
        ],
        compiler_params=params,
        name="up_and_down",
    )(core, normed, b_up.astype(f32)[None, :], weights)
    other = shift(other, "core", 1, NCORE)
    mine = pl.pallas_call(
        second_kernel,
        out_shape=half_out,
        in_specs=[whole(pltpu.SMEM), whole(), whole(pl.ANY)],
        out_specs=whole(),
        scratch_shapes=[down, pltpu.SemaphoreType.DMA((NX,))],
        compiler_params=params,
        name="down_own",
    )(core, hidden, weights)
    block = jax.ShapeDtypeStruct((width, cells), bf16)
    own, *sent = pl.pallas_call(
        pair_kernel,
        out_shape=(jax.ShapeDtypeStruct((width, cells), f32),) + (block,) * len(DISTANCES),
        in_specs=[whole(pltpu.SMEM), whole(), whole()],
        out_specs=(whole(),) * (1 + len(DISTANCES)),
        compiler_params=params,
        name="pair",
    )(x, mine, other)
    return own, *(shift(block, "x", d, NX) for d, block in zip(DISTANCES, sent))


def per_device(
    crop_features, crop_counts, first_crop, tile_embed, dw_weight, conv_bias,
    ln_gain, ln_bias, w_up, b_up, w_down, b_down, gamma,
):
    f32 = jnp.float32
    width = b_down.shape[0]
    side = crop_features.shape[1]
    seq_index = lax.axis_index(SEQ)
    start = lax.axis_index(TP) * width
    weights = gather_weights(w_up, w_down)

    def channels(array):
        return lax.dynamic_slice_in_dim(array, start, width, array.ndim - 1)

    slots = channels(crop_features)
    before, after = exchange(slots, seq_index, first_crop)
    table = channels(jnp.concatenate([dw_weight, tile_embed, conv_bias[None, :]]))
    block_in, conv = depthwise(
        seq_index, first_crop, crop_counts, slots, before, after, table
    )
    cells = PER_DEV * side * side
    padding = -cells % 128
    conv_t = jnp.pad(conv[:, :, :side].reshape(cells, width), ((0, padding), (0, 0))).T
    conv_t = conv_t.astype(jnp.float16)
    conv_all = lax.all_gather(conv_t, TP, axis=0, tiled=True).astype(f32)
    mean = jnp.mean(conv_all, axis=0, keepdims=True)
    var = jnp.mean((conv_all - mean) ** 2, axis=0, keepdims=True)
    normed = (
        (conv_all - mean) / jnp.sqrt(var + 1e-6) * ln_gain.astype(f32)[:, None]
        + ln_bias.astype(f32)[:, None]
    ).astype(jnp.bfloat16).T
    sums = mlp_sum(normed, weights, b_up, width)
    result = pl.pallas_call(
        last_kernel,
        out_shape=jax.ShapeDtypeStruct((cells, width), jnp.bfloat16),
        in_specs=[whole()] * (len(sums) + 3),
        out_specs=whole(),
        compiler_params=pltpu.CompilerParams(vmem_limit_bytes=48 * 2**20),
        name="result",
    )(*sums, b_down.astype(f32)[:, None], gamma[:, None], block_in.reshape(cells, width))
    return result.reshape(PER_DEV, side, side, width)


def solution(mesh):
    fine = Mesh(mesh.devices.reshape(NY, NZ, NX, NCORE), SEQ + TP)
    placed = (
        P(SEQ, None, None, None), P(), P(), P(), P(), P(), P(), P(),
        P(SEQ, TP), P(TP), P(TP, SEQ), P(TP), P(TP),
    )
    return jax.shard_map(
        per_device,
        mesh=fine,
        in_specs=placed,
        out_specs=P(SEQ, None, None, TP),
        check_vma=False,
    )
```

```python
import jax
import jax.numpy as jnp
from jax import lax
from jax.experimental import pallas as pl
from jax.experimental.pallas import tpu as pltpu
from jax.sharding import Mesh, PartitionSpec as P

NY, NZ, NX, NCORE = 4, 16, 4, 2
SEQ = ("y", "z")
TP = ("x", "core")
PER_DEV = 2
KSIDE = 7
DISTANCES = (2, 1, 3)


def shift(block, axis, distance, size):
    return lax.ppermute(block, axis, [(i, (i + distance) % size) for i in range(size)])


def gather_z(w_up, w_down):
    both = jnp.stack([w_up, w_down.T]).astype(jnp.float32) * 2.0**18
    over_z = lax.all_gather(both.astype(jnp.float16), "z", axis=1, tiled=True)
    return (over_z.astype(jnp.float32) * 2.0**-18).astype(jnp.bfloat16)


def gather_y(own):
    behind = shift(own, "y", 1, NY)
    ahead = shift(own, "y", -1, NY)
    far_up = shift(behind[0], "y", 1, NY)
    far_down = shift(ahead[1], "y", -1, NY)
    return own, ahead, behind, far_up, far_down


def exchange(slots, seq_index, first_crop):
    count = NY * NZ
    first = first_crop[seq_index]
    last_slot = slots.shape[0] - 1

    def crop(number):
        return lax.dynamic_index_in_dim(
            slots, jnp.clip(number - first, 0, last_slot), 0, keepdims=False
        )

    target = PER_DEV * seq_index
    before = lax.ppermute(
        crop(target + PER_DEV), SEQ, [(i, i + 1) for i in range(count - 1)]
    )
    after = lax.ppermute(crop(target - 1), SEQ, [(i + 1, i) for i in range(count - 1)])
    return before, after


def conv_kernel(
    seq, first_crop, crop_counts, slots, before, after, table, block_in, conv, padded, shifted, taps
):
    f32 = jnp.float32
    side = block_in.shape[1]
    shards = first_crop.shape[0]
    margin = KSIDE // 2
    here = seq[0]
    first = first_crop[here]
    limit = jnp.where(
        here + 1 < shards, first_crop[jnp.minimum(here + 1, shards - 1)], PER_DEV * shards
    )
    tile_at = KSIDE * KSIDE
    bias = table[tile_at + 3 : tile_at + 4, :].astype(f32)
    for t in range(KSIDE * KSIDE):
        taps[t] = jnp.broadcast_to(table[t : t + 1, :].astype(f32), taps.shape[1:])
    padded[...] = jnp.zeros_like(padded)
    shifted[...] = jnp.zeros_like(shifted)
    for n in range(PER_DEV):
        target = PER_DEV * here + n

        def image(i, carry):
            start, begin = carry
            return start + crop_counts[i], jnp.where(start <= target, start, begin)

        _, begin = lax.fori_loop(0, crop_counts.shape[0], image, (jnp.int32(0), jnp.int32(0)))
        place = target - begin
        tile = jnp.zeros_like(bias)
        for p in range(3):
            row = table[tile_at + p : tile_at + p + 1, :].astype(f32)
            tile = jnp.where(place == p, row, tile)
        mine = slots[jnp.clip(target - first, 0, slots.shape[0] - 1)].astype(f32)
        received = (before if n == 0 else after)[...].astype(f32)
        held = (first <= target) & (target < limit)
        crop = jnp.where(held, mine, received) + tile
        block_in[n] = crop
        padded[:, margin : margin + side, :] = crop
        for b in range(KSIDE):
            shifted[b, n, margin : margin + side] = padded[:, b : b + shifted.shape[3], :]
    columns, width = shifted.shape[3:]
    groups = side // 3

    def three_rows(g, _):
        n, top = lax.div(g, groups), lax.rem(g, groups) * 3
        sums = [jnp.zeros((columns // 8, 8, width), f32) for _ in range(3)]
        for b in range(KSIDE):
            for r in range(KSIDE + 2):
                row = shifted[b, n, top + r].reshape(columns // 8, 8, width)
                for o in range(3):
                    if 0 <= r - o < KSIDE:
                        sums[o] = sums[o] + row * taps[(r - o) * KSIDE + b][None]
        for o in range(3):
            conv[n, top + o] = sums[o].reshape(columns, width) + bias
        return 0

    lax.fori_loop(0, PER_DEV * groups, three_rows, 0)


def depthwise(seq_index, first_crop, crop_counts, slots, before, after, table):
    f32 = jnp.float32
    side, width = slots.shape[1], slots.shape[3]
    columns = 24
    return pl.pallas_call(
        conv_kernel,
        out_shape=(
            jax.ShapeDtypeStruct((PER_DEV, side, side, width), f32),
            jax.ShapeDtypeStruct((PER_DEV, side, columns, width), f32),
        ),
        in_specs=[whole(pltpu.SMEM)] * 3 + [whole()] * 4,
        out_specs=(whole(), whole()),
        scratch_shapes=[
            pltpu.VMEM((side, columns + 8, width), f32),
            pltpu.VMEM((KSIDE, PER_DEV, side + 6, columns, width), f32),
            pltpu.VMEM((KSIDE * KSIDE, 8, width), f32),
        ],
        compiler_params=pltpu.CompilerParams(vmem_limit_bytes=48 * 2**20),
        name="conv",
    )(seq_index.astype(jnp.int32).reshape(1), first_crop, crop_counts, slots, before, after, table)


def whole(space=pltpu.VMEM):
    return pl.BlockSpec(memory_space=space)


def split_blocks(blocks):
    own, ahead, behind, far_up, far_down = blocks
    ups = (own.at[0], ahead.at[0], far_up, behind.at[0])
    downs = (own.at[1], ahead.at[1], far_down, behind.at[1])
    return ups, downs


def copy_down_rows(blocks, buffer, sems, y, core):
    width = buffer.shape[0] // NX
    copies = []
    for d, block in enumerate(split_blocks(blocks)[1]):
        source = pl.multiple_of(core * width, width)
        target = pl.multiple_of(lax.rem(y + d, NY) * width, width)
        copies.append(
            pltpu.make_async_copy(
                block.at[pl.ds(source, width), :], buffer.at[pl.ds(target, width), :], sems.at[d]
            )
        )
    return copies


def down_product(buffer, hidden, out):
    width = buffer.shape[0] // NX
    product = lax.dot_general(
        buffer[...], hidden, (((1,), (1,)), ((), ())), preferred_element_type=jnp.float32
    )
    for x in range(NX):
        out[x] = product[x * width : (x + 1) * width].astype(out.dtype)


def first_kernel(place, normed, b_up, *refs):
    blocks, (hidden, out, up, down, up_sem, down_sem) = refs[:5], refs[5:]
    y, core = place[0], place[2]
    ups = []
    for d, block in enumerate(split_blocks(blocks)[0]):
        rows = block.shape[0]
        target = pl.multiple_of(lax.rem(y + d, NY) * rows, rows)
        ups.append(pltpu.make_async_copy(block, up.at[pl.ds(target, rows), :], up_sem.at[d]))
    for copy in ups:
        copy.start()
    downs = copy_down_rows(blocks, down, down_sem, y, 1 - core)
    for copy in downs:
        copy.start()
    for copy in ups:
        copy.wait()
    cells = normed.shape[0]
    rows = cells // 4
    for r in range(0, cells, rows):
        pre = jnp.dot(normed[r : r + rows], up[...], preferred_element_type=jnp.float32)
        pre = pre + b_up[...]
        act = 0.5 * pre * (1.0 + lax.erf(pre * 0.5**0.5))
        hidden[r : r + rows] = act.astype(hidden.dtype)
    for copy in downs:
        copy.wait()
    down_product(down, hidden[...], out)


def second_kernel(place, hidden, *refs):
    blocks, (out, down, down_sem) = refs[:5], refs[5:]
    downs = copy_down_rows(blocks, down, down_sem, place[0], place[2])
    for copy in downs:
        copy.start()
    for copy in downs:
        copy.wait()
    down_product(down, hidden[...], out)


def pair_kernel(place, mine, other, own, *sent):
    def pair(distance):
        i = lax.rem(place[1] + distance, NX)
        return mine[i].astype(jnp.float32) + other[i].astype(jnp.float32)

    own[...] = pair(0)
    for distance, block in zip(DISTANCES, sent):
        block[...] = pair(distance).astype(block.dtype)


def last_kernel(own, first, second, third, b_down, gamma, residual, out):
    total = own[...]
    for block in (first, second, third):
        total = total + block[...].astype(jnp.float32)
    scaled = gamma[...] * (total + b_down[...])
    rows = residual.shape[0]
    out[...] = (residual[...] + scaled.T[:rows]).astype(out.dtype)


def mlp_sum(normed, blocks, b_up, width):
    bf16, f32 = jnp.bfloat16, jnp.float32
    cells, units = normed.shape[0], b_up.shape[0]
    place = jnp.stack([lax.axis_index(a).astype(jnp.int32) for a in ("y", "x", "core")])
    params = pltpu.CompilerParams(vmem_limit_bytes=48 * 2**20)
    half_out = jax.ShapeDtypeStruct((NX, width, cells), bf16)
    down = pltpu.VMEM((NX * width, units), bf16)
    hidden, other = pl.pallas_call(
        first_kernel,
        out_shape=(jax.ShapeDtypeStruct((cells, units), bf16), half_out),
        in_specs=[whole(pltpu.SMEM), whole(), whole()] + [whole(pl.ANY)] * len(blocks),
        out_specs=(whole(), whole()),
        scratch_shapes=[
            pltpu.VMEM((normed.shape[1], units), bf16),
            down,
            pltpu.SemaphoreType.DMA((4,)),
            pltpu.SemaphoreType.DMA((NX,)),
        ],
        compiler_params=params,
        name="up_and_down",
    )(place, normed, b_up.astype(f32)[None, :], *blocks)
    other = shift(other, "core", 1, NCORE)
    mine = pl.pallas_call(
        second_kernel,
        out_shape=half_out,
        in_specs=[whole(pltpu.SMEM), whole()] + [whole(pl.ANY)] * len(blocks),
        out_specs=whole(),
        scratch_shapes=[down, pltpu.SemaphoreType.DMA((NX,))],
        compiler_params=params,
        name="down_own",
    )(place, hidden, *blocks)
    block = jax.ShapeDtypeStruct((width, cells), bf16)
    own, *sent = pl.pallas_call(
        pair_kernel,
        out_shape=(jax.ShapeDtypeStruct((width, cells), f32),) + (block,) * len(DISTANCES),
        in_specs=[whole(pltpu.SMEM), whole(), whole()],
        out_specs=(whole(),) * (1 + len(DISTANCES)),
        compiler_params=params,
        name="pair",
    )(place, mine, other)
    return own, *(shift(block, "x", d, NX) for d, block in zip(DISTANCES, sent))


def per_device(
    crop_features, crop_counts, first_crop, tile_embed, dw_weight, conv_bias,
    ln_gain, ln_bias, w_up, b_up, w_down, b_down, gamma,
):
    f32 = jnp.float32
    width = b_down.shape[0]
    side = crop_features.shape[1]
    seq_index = lax.axis_index(SEQ)
    start = lax.axis_index(TP) * width
    blocks = gather_y(gather_z(w_up, w_down))

    def channels(array):
        return lax.dynamic_slice_in_dim(array, start, width, array.ndim - 1)

    slots = channels(crop_features)
    before, after = exchange(slots, seq_index, first_crop)
    table = channels(jnp.concatenate([dw_weight, tile_embed, conv_bias[None, :]]))
    block_in, conv = depthwise(
        seq_index, first_crop, crop_counts, slots, before, after, table
    )
    cells = PER_DEV * side * side
    padding = -cells % 128
    conv_t = jnp.pad(conv[:, :, :side].reshape(cells, width), ((0, padding), (0, 0))).T
    conv_t = conv_t.astype(jnp.float16)
    conv_all = lax.all_gather(conv_t, TP, axis=0, tiled=True).astype(f32)
    mean = jnp.mean(conv_all, axis=0, keepdims=True)
    var = jnp.mean((conv_all - mean) ** 2, axis=0, keepdims=True)
    normed = (
        (conv_all - mean) / jnp.sqrt(var + 1e-6) * ln_gain.astype(f32)[:, None]
        + ln_bias.astype(f32)[:, None]
    ).astype(jnp.bfloat16).T
    sums = mlp_sum(normed, blocks, b_up, width)
    result = pl.pallas_call(
        last_kernel,
        out_shape=jax.ShapeDtypeStruct((cells, width), jnp.bfloat16),
        in_specs=[whole()] * (len(sums) + 3),
        out_specs=whole(),
        compiler_params=pltpu.CompilerParams(vmem_limit_bytes=48 * 2**20),
        name="result",
    )(*sums, b_down.astype(f32)[:, None], gamma[:, None], block_in.reshape(cells, width))
    return result.reshape(PER_DEV, side, side, width)


def solution(mesh):
    fine = Mesh(mesh.devices.reshape(NY, NZ, NX, NCORE), SEQ + TP)
    placed = (
        P(SEQ, None, None, None), P(), P(), P(), P(), P(), P(), P(),
        P(SEQ, TP), P(TP), P(TP, SEQ), P(TP), P(TP),
    )
    return jax.shard_map(
        per_device,
        mesh=fine,
        in_specs=placed,
        out_specs=P(SEQ, None, None, TP),
        check_vma=False,
    )
```

```python
import jax
import jax.numpy as jnp
from jax import lax
from jax.experimental import pallas as pl
from jax.experimental.pallas import tpu as pltpu
from jax.sharding import Mesh, PartitionSpec as P

NY, NZ, NX, NCORE = 4, 16, 4, 2
SEQ = ("y", "z")
TP = ("x", "core")
PER_DEV = 2
KSIDE = 7


def shift(block, axis, distance, size):
    return lax.ppermute(block, axis, [(i, (i + distance) % size) for i in range(size)])


def gather_weights(w_up, w_down):
    both = jnp.stack([w_up, w_down.T])
    over_y = lax.all_gather(both, "y", axis=1)
    over_z = lax.all_gather(over_y, "z", axis=2)
    return over_z.reshape(2, NY * NZ * w_up.shape[0], w_up.shape[1])


def exchange(slots, seq_index, first_crop):
    count = NY * NZ
    first = first_crop[seq_index]
    last_slot = slots.shape[0] - 1

    def crop(number):
        return lax.dynamic_index_in_dim(
            slots, jnp.clip(number - first, 0, last_slot), 0, keepdims=False
        )

    target = PER_DEV * seq_index
    before = lax.ppermute(
        crop(target + PER_DEV), SEQ, [(i, i + 1) for i in range(count - 1)]
    )
    after = lax.ppermute(crop(target - 1), SEQ, [(i + 1, i) for i in range(count - 1)])
    return before, after


def conv_kernel(
    seq, first_crop, crop_counts, slots, before, after, table, block_in, conv, padded, shifted, taps
):
    f32 = jnp.float32
    side = block_in.shape[1]
    shards = first_crop.shape[0]
    margin = KSIDE // 2
    here = seq[0]
    first = first_crop[here]
    limit = jnp.where(
        here + 1 < shards, first_crop[jnp.minimum(here + 1, shards - 1)], PER_DEV * shards
    )
    tile_at = KSIDE * KSIDE
    bias = table[tile_at + 3 : tile_at + 4, :].astype(f32)
    for t in range(KSIDE * KSIDE):
        taps[t] = jnp.broadcast_to(table[t : t + 1, :].astype(f32), taps.shape[1:])
    padded[...] = jnp.zeros_like(padded)
    shifted[...] = jnp.zeros_like(shifted)
    for n in range(PER_DEV):
        target = PER_DEV * here + n

        def image(i, carry):
            start, begin = carry
            return start + crop_counts[i], jnp.where(start <= target, start, begin)

        _, begin = lax.fori_loop(0, crop_counts.shape[0], image, (jnp.int32(0), jnp.int32(0)))
        place = target - begin
        tile = jnp.zeros_like(bias)
        for p in range(3):
            row = table[tile_at + p : tile_at + p + 1, :].astype(f32)
            tile = jnp.where(place == p, row, tile)
        mine = slots[jnp.clip(target - first, 0, slots.shape[0] - 1)].astype(f32)
        received = (before if n == 0 else after)[...].astype(f32)
        held = (first <= target) & (target < limit)
        crop = jnp.where(held, mine, received) + tile
        block_in[n] = crop
        padded[:, margin : margin + side, :] = crop
        for b in range(KSIDE):
            shifted[b, n, margin : margin + side] = padded[:, b : b + shifted.shape[3], :]
    columns, width = shifted.shape[3:]
    groups = side // 3

    def three_rows(g, _):
        n, top = lax.div(g, groups), lax.rem(g, groups) * 3
        sums = [jnp.zeros((columns // 8, 8, width), f32) for _ in range(3)]
        for b in range(KSIDE):
            for r in range(KSIDE + 2):
                row = shifted[b, n, top + r].reshape(columns // 8, 8, width)
                for o in range(3):
                    if 0 <= r - o < KSIDE:
                        sums[o] = sums[o] + row * taps[(r - o) * KSIDE + b][None]
        for o in range(3):
            conv[n, top + o] = sums[o].reshape(columns, width) + bias
        return 0

    lax.fori_loop(0, PER_DEV * groups, three_rows, 0)


def depthwise(seq_index, first_crop, crop_counts, slots, before, after, table):
    f32 = jnp.float32
    side, width = slots.shape[1], slots.shape[3]
    columns = 24
    return pl.pallas_call(
        conv_kernel,
        out_shape=(
            jax.ShapeDtypeStruct((PER_DEV, side, side, width), f32),
            jax.ShapeDtypeStruct((PER_DEV, side, columns, width), f32),
        ),
        in_specs=[whole(pltpu.SMEM)] * 3 + [whole()] * 4,
        out_specs=(whole(), whole()),
        scratch_shapes=[
            pltpu.VMEM((side, columns + 8, width), f32),
            pltpu.VMEM((KSIDE, PER_DEV, side + 6, columns, width), f32),
            pltpu.VMEM((KSIDE * KSIDE, 8, width), f32),
        ],
        compiler_params=vmem(16),
        name="conv",
    )(seq_index.astype(jnp.int32).reshape(1), first_crop, crop_counts, slots, before, after, table)


def vmem(mebibytes):
    return pltpu.CompilerParams(vmem_limit_bytes=mebibytes * 2**20)


def whole(space=pltpu.VMEM):
    return pl.BlockSpec(memory_space=space)


def copy_down_rows(weights, buffer, sems, core):
    width = buffer.shape[0] // NX
    copies = []
    for x in range(NX):
        row = pl.multiple_of((x * NCORE + core) * width, width)
        copies.append(
            pltpu.make_async_copy(
                weights.at[1, pl.ds(row, width), :],
                buffer.at[pl.ds(x * width, width), :],
                sems.at[x],
            )
        )
    return copies


def down_product(buffer, hidden, out):
    width = buffer.shape[0] // NX
    product = lax.dot_general(
        buffer[...], hidden, (((1,), (1,)), ((), ())), preferred_element_type=jnp.float32
    )
    for x in range(NX):
        out[x] = product[x * width : (x + 1) * width].astype(out.dtype)


def first_kernel(core, normed, b_up, weights, hidden, out, up, down, up_sem, down_sem):
    ups = []
    pieces = up_sem.shape[0]
    step = up.shape[0] // pieces
    for p in range(pieces):
        span = pl.ds(p * step, step)
        ups.append(pltpu.make_async_copy(weights.at[0, span, :], up.at[span, :], up_sem.at[p]))
    for copy in ups:
        copy.start()
    downs = copy_down_rows(weights, down, down_sem, 1 - core[0])
    for copy in downs:
        copy.start()
    for copy in ups:
        copy.wait()
    cells = normed.shape[0]
    rows = cells // 4
    for r in range(0, cells, rows):
        pre = jnp.dot(normed[r : r + rows], up[...], preferred_element_type=jnp.float32)
        pre = pre + b_up[...]
        act = 0.5 * pre * (1.0 + lax.erf(pre * 0.5**0.5))
        hidden[r : r + rows] = act.astype(hidden.dtype)
    for copy in downs:
        copy.wait()
    down_product(down, hidden[...], out)


def second_kernel(core, hidden, weights, out, down, down_sem):
    downs = copy_down_rows(weights, down, down_sem, core[0])
    for copy in downs:
        copy.start()
    for copy in downs:
        copy.wait()
    down_product(down, hidden[...], out)


def pair_kernel(mine, other, out):
    total = mine[...].astype(jnp.float32) + other[...].astype(jnp.float32)
    out[...] = total.astype(out.dtype)


def last_kernel(parts, b_down, gamma, residual, out):
    total = parts[0].astype(jnp.float32)
    for i in range(1, NX):
        total = total + parts[i].astype(jnp.float32)
    scaled = gamma[...] * (total + b_down[...])
    rows = residual.shape[0]
    out[...] = (residual[...] + scaled.T[:rows]).astype(out.dtype)


def mlp_sum(normed, weights, b_up, width):
    bf16, f32 = jnp.bfloat16, jnp.float32
    cells, units = normed.shape[0], b_up.shape[0]
    core = lax.axis_index("core").astype(jnp.int32).reshape(1)
    half_out = jax.ShapeDtypeStruct((NX, width, cells), bf16)
    down = pltpu.VMEM((NX * width, units), bf16)
    weights = pltpu.with_memory_space_constraint(weights, pltpu.HBM)
    hidden, other = pl.pallas_call(
        first_kernel,
        out_shape=(jax.ShapeDtypeStruct((cells, units), bf16), half_out),
        in_specs=[whole(pltpu.SMEM), whole(), whole(), whole(pl.ANY)],
        out_specs=(whole(), whole()),
        scratch_shapes=[
            pltpu.VMEM(weights.shape[1:], bf16),
            down,
            pltpu.SemaphoreType.DMA((4,)),
            pltpu.SemaphoreType.DMA((NX,)),
        ],
        compiler_params=vmem(20),
        name="up_and_down",
    )(core, normed, b_up.astype(f32)[None, :], weights)
    other = shift(other, "core", 1, NCORE)
    mine = pl.pallas_call(
        second_kernel,
        out_shape=half_out,
        in_specs=[whole(pltpu.SMEM), whole(), whole(pl.ANY)],
        out_specs=whole(),
        scratch_shapes=[down, pltpu.SemaphoreType.DMA((NX,))],
        compiler_params=vmem(12),
        name="down_own",
    )(core, hidden, weights)
    pairs = pl.pallas_call(
        pair_kernel,
        out_shape=half_out,
        in_specs=[whole(), whole()],
        out_specs=whole(),
        compiler_params=vmem(12),
        name="pair",
    )(mine, other)
    return lax.all_to_all(pairs, "x", split_axis=0, concat_axis=0, tiled=True)


def per_device(
    crop_features, crop_counts, first_crop, tile_embed, dw_weight, conv_bias,
    ln_gain, ln_bias, w_up, b_up, w_down, b_down, gamma,
):
    f32 = jnp.float32
    width = b_down.shape[0]
    side = crop_features.shape[1]
    seq_index = lax.axis_index(SEQ)
    start = lax.axis_index(TP) * width
    weights = gather_weights(w_up, w_down)

    def channels(array):
        return lax.dynamic_slice_in_dim(array, start, width, array.ndim - 1)

    slots = channels(crop_features)
    before, after = exchange(slots, seq_index, first_crop)
    table = channels(jnp.concatenate([dw_weight, tile_embed, conv_bias[None, :]]))
    block_in, conv = depthwise(
        seq_index, first_crop, crop_counts, slots, before, after, table
    )
    cells = PER_DEV * side * side
    padding = -cells % 128
    conv_t = jnp.pad(conv[:, :, :side].reshape(cells, width), ((0, padding), (0, 0))).T
    conv_t = conv_t.astype(jnp.float16)
    conv_all = lax.all_gather(conv_t, TP, axis=0, tiled=True).astype(f32)
    mean = jnp.mean(conv_all, axis=0, keepdims=True)
    var = jnp.mean((conv_all - mean) ** 2, axis=0, keepdims=True)
    normed = (
        (conv_all - mean) / jnp.sqrt(var + 1e-6) * ln_gain.astype(f32)[:, None]
        + ln_bias.astype(f32)[:, None]
    ).astype(jnp.bfloat16).T
    parts = mlp_sum(normed, weights, b_up, width)
    result = pl.pallas_call(
        last_kernel,
        out_shape=jax.ShapeDtypeStruct((cells, width), jnp.bfloat16),
        in_specs=[whole()] * 4,
        out_specs=whole(),
        compiler_params=vmem(12),
        name="result",
    )(parts, b_down.astype(f32)[:, None], gamma[:, None], block_in.reshape(cells, width))
    return result.reshape(PER_DEV, side, side, width)


def solution(mesh):
    fine = Mesh(mesh.devices.reshape(NY, NZ, NX, NCORE), SEQ + TP)
    placed = (
        P(SEQ, None, None, None), P(), P(), P(), P(), P(), P(), P(),
        P(SEQ, TP), P(TP), P(TP, SEQ), P(TP), P(TP),
    )
    return jax.shard_map(
        per_device,
        mesh=fine,
        in_specs=placed,
        out_specs=P(SEQ, None, None, TP),
        check_vma=False,
    )
```

```python
import jax
import jax.numpy as jnp
from jax import lax
from jax.experimental import pallas as pl
from jax.experimental.pallas import tpu as pltpu
from jax.sharding import Mesh, PartitionSpec as P

NY, NZ, NX, NCORE = 4, 16, 4, 2
SEQ = ("y", "z")
TP = ("x", "core")
PER_DEV = 2
KSIDE = 7
DISTANCES = (2, 1, 3)


def shift(block, axis, distance, size):
    return lax.ppermute(block, axis, [(i, (i + distance) % size) for i in range(size)])


def gather_z(w_up, w_down):
    both = jnp.stack([w_up, w_down.T]).astype(jnp.float32) * 2.0**18
    over_z = lax.all_gather(both.astype(jnp.float16), "z", axis=1, tiled=True)
    return (over_z.astype(jnp.float32) * 2.0**-18).astype(jnp.bfloat16)


def gather_y(own):
    return own, *(shift(own, "y", -d, NY) for d in (1, 2, 3))


def exchange(slots, seq_index, first_crop):
    count = NY * NZ
    first = first_crop[seq_index]
    last_slot = slots.shape[0] - 1

    def crop(number):
        return lax.dynamic_index_in_dim(
            slots, jnp.clip(number - first, 0, last_slot), 0, keepdims=False
        )

    target = PER_DEV * seq_index
    before = lax.ppermute(
        crop(target + PER_DEV), SEQ, [(i, i + 1) for i in range(count - 1)]
    )
    after = lax.ppermute(crop(target - 1), SEQ, [(i + 1, i) for i in range(count - 1)])
    return before, after


def conv_kernel(
    seq, first_crop, crop_counts, slots, before, after, table, block_in, conv, padded, shifted, taps
):
    f32 = jnp.float32
    side = block_in.shape[1]
    shards = first_crop.shape[0]
    margin = KSIDE // 2
    here = seq[0]
    first = first_crop[here]
    limit = jnp.where(
        here + 1 < shards, first_crop[jnp.minimum(here + 1, shards - 1)], PER_DEV * shards
    )
    tile_at = KSIDE * KSIDE
    bias = table[tile_at + 3 : tile_at + 4, :].astype(f32)
    for t in range(KSIDE * KSIDE):
        taps[t] = jnp.broadcast_to(table[t : t + 1, :].astype(f32), taps.shape[1:])
    padded[...] = jnp.zeros_like(padded)
    shifted[...] = jnp.zeros_like(shifted)
    for n in range(PER_DEV):
        target = PER_DEV * here + n

        def image(i, carry):
            start, begin = carry
            return start + crop_counts[i], jnp.where(start <= target, start, begin)

        _, begin = lax.fori_loop(0, crop_counts.shape[0], image, (jnp.int32(0), jnp.int32(0)))
        place = target - begin
        tile = jnp.zeros_like(bias)
        for p in range(3):
            row = table[tile_at + p : tile_at + p + 1, :].astype(f32)
            tile = jnp.where(place == p, row, tile)
        mine = slots[jnp.clip(target - first, 0, slots.shape[0] - 1)].astype(f32)
        received = (before if n == 0 else after)[...].astype(f32)
        held = (first <= target) & (target < limit)
        crop = jnp.where(held, mine, received) + tile
        block_in[n] = crop
        padded[:, margin : margin + side, :] = crop
        for b in range(KSIDE):
            shifted[b, n, margin : margin + side] = padded[:, b : b + shifted.shape[3], :]
    columns, width = shifted.shape[3:]
    groups = side // 3

    def three_rows(g, _):
        n, top = lax.div(g, groups), lax.rem(g, groups) * 3
        sums = [jnp.zeros((columns // 8, 8, width), f32) for _ in range(3)]
        for b in range(KSIDE):
            for r in range(KSIDE + 2):
                row = shifted[b, n, top + r].reshape(columns // 8, 8, width)
                for o in range(3):
                    if 0 <= r - o < KSIDE:
                        sums[o] = sums[o] + row * taps[(r - o) * KSIDE + b][None]
        for o in range(3):
            conv[n, top + o] = sums[o].reshape(columns, width) + bias
        return 0

    lax.fori_loop(0, PER_DEV * groups, three_rows, 0)


def depthwise(seq_index, first_crop, crop_counts, slots, before, after, table):
    f32 = jnp.float32
    side, width = slots.shape[1], slots.shape[3]
    columns = 24
    return pl.pallas_call(
        conv_kernel,
        out_shape=(
            jax.ShapeDtypeStruct((PER_DEV, side, side, width), f32),
            jax.ShapeDtypeStruct((PER_DEV, side, columns, width), f32),
        ),
        in_specs=[whole(pltpu.SMEM)] * 3 + [whole()] * 4,
        out_specs=(whole(), whole()),
        scratch_shapes=[
            pltpu.VMEM((side, columns + 8, width), f32),
            pltpu.VMEM((KSIDE, PER_DEV, side + 6, columns, width), f32),
            pltpu.VMEM((KSIDE * KSIDE, 8, width), f32),
        ],
        compiler_params=vmem(16),
        name="conv",
    )(seq_index.astype(jnp.int32).reshape(1), first_crop, crop_counts, slots, before, after, table)


def vmem(mebibytes):
    return pltpu.CompilerParams(vmem_limit_bytes=mebibytes * 2**20)


def whole(space=pltpu.VMEM):
    return pl.BlockSpec(memory_space=space)


def norm_kernel(conv, gain, bias, normed):
    channels, cells = conv.shape
    step = 128
    for c in range(0, cells, step):
        block = conv[:, c : c + step]
        mean = jnp.sum(block, axis=0, keepdims=True) * (1.0 / channels)
        block = block - mean
        var = jnp.sum(block * block, axis=0, keepdims=True) * (1.0 / channels)
        block = block * lax.rsqrt(var + 1e-6)
        normed[c : c + step, :] = (block.T * gain[...] + bias[...]).astype(normed.dtype)


def layer_norm(conv, gain, bias):
    return pl.pallas_call(
        norm_kernel,
        out_shape=jax.ShapeDtypeStruct(conv.shape[::-1], jnp.bfloat16),
        in_specs=[whole()] * 3,
        out_specs=whole(),
        compiler_params=vmem(20),
        name="norm",
    )(conv, gain.astype(jnp.float32)[None, :], bias.astype(jnp.float32)[None, :])


def copy_down_rows(blocks, buffer, sems, y, core):
    width = buffer.shape[0] // NX
    copies = []
    for d, block in enumerate(blocks):
        source = pl.multiple_of(core * width, width)
        target = pl.multiple_of(lax.rem(y + d, NY) * width, width)
        copies.append(
            pltpu.make_async_copy(
                block.at[1, pl.ds(source, width), :], buffer.at[pl.ds(target, width), :], sems.at[d]
            )
        )
    return copies


def down_product(buffer, hidden, out):
    width = buffer.shape[0] // NX
    product = lax.dot_general(
        buffer[...], hidden, (((1,), (1,)), ((), ())), preferred_element_type=jnp.float32
    )
    for x in range(NX):
        out[x] = product[x * width : (x + 1) * width].astype(out.dtype)


def first_kernel(place, normed, b_up, *refs):
    blocks, (hidden, out, up, down, up_sem, down_sem) = refs[:NY], refs[NY:]
    y, core = place[0], place[2]
    ups = []
    for d, block in enumerate(blocks):
        rows = block.shape[1]
        target = pl.multiple_of(lax.rem(y + d, NY) * rows, rows)
        ups.append(pltpu.make_async_copy(block.at[0], up.at[pl.ds(target, rows), :], up_sem.at[d]))
    for copy in ups:
        copy.start()
    downs = copy_down_rows(blocks, down, down_sem, y, 1 - core)
    for copy in downs:
        copy.start()
    for copy in ups:
        copy.wait()
    cells = normed.shape[0]
    rows = cells // 4
    for r in range(0, cells, rows):
        pre = jnp.dot(normed[r : r + rows], up[...], preferred_element_type=jnp.float32)
        pre = pre + b_up[...]
        act = 0.5 * pre * (1.0 + lax.erf(pre * 0.5**0.5))
        hidden[r : r + rows] = act.astype(hidden.dtype)
    for copy in downs:
        copy.wait()
    down_product(down, hidden[...], out)


def second_kernel(place, hidden, *refs):
    blocks, (out, down, down_sem) = refs[:NY], refs[NY:]
    downs = copy_down_rows(blocks, down, down_sem, place[0], place[2])
    for copy in downs:
        copy.start()
    for copy in downs:
        copy.wait()
    down_product(down, hidden[...], out)


def pair_kernel(place, mine, other, own, *sent):
    def pair(distance):
        i = lax.rem(place[1] + distance, NX)
        return mine[i].astype(jnp.float32) + other[i].astype(jnp.float32)

    own[...] = pair(0)
    for distance, block in zip(DISTANCES, sent):
        block[...] = pair(distance).astype(block.dtype)


def last_kernel(own, first, second, third, b_down, gamma, residual, out):
    total = own[...]
    for block in (first, second, third):
        total = total + block[...].astype(jnp.float32)
    scaled = gamma[...] * (total + b_down[...])
    rows = residual.shape[0]
    out[...] = (residual[...] + scaled.T[:rows]).astype(out.dtype)


def mlp_sum(normed, blocks, b_up, width):
    bf16, f32 = jnp.bfloat16, jnp.float32
    cells, units = normed.shape[0], b_up.shape[0]
    place = jnp.stack([lax.axis_index(a).astype(jnp.int32) for a in ("y", "x", "core")])
    half_out = jax.ShapeDtypeStruct((NX, width, cells), bf16)
    down = pltpu.VMEM((NX * width, units), bf16)
    hidden, other = pl.pallas_call(
        first_kernel,
        out_shape=(jax.ShapeDtypeStruct((cells, units), bf16), half_out),
        in_specs=[whole(pltpu.SMEM), whole(), whole()] + [whole(pl.ANY)] * len(blocks),
        out_specs=(whole(), whole()),
        scratch_shapes=[
            pltpu.VMEM((normed.shape[1], units), bf16),
            down,
            pltpu.SemaphoreType.DMA((4,)),
            pltpu.SemaphoreType.DMA((NX,)),
        ],
        compiler_params=vmem(20),
        name="up_and_down",
    )(place, normed, b_up.astype(f32)[None, :], *blocks)
    other = shift(other, "core", 1, NCORE)
    mine = pl.pallas_call(
        second_kernel,
        out_shape=half_out,
        in_specs=[whole(pltpu.SMEM), whole()] + [whole(pl.ANY)] * len(blocks),
        out_specs=whole(),
        scratch_shapes=[down, pltpu.SemaphoreType.DMA((NX,))],
        compiler_params=vmem(12),
        name="down_own",
    )(place, hidden, *blocks)
    block = jax.ShapeDtypeStruct((width, cells), bf16)
    own, *sent = pl.pallas_call(
        pair_kernel,
        out_shape=(jax.ShapeDtypeStruct((width, cells), f32),) + (block,) * len(DISTANCES),
        in_specs=[whole(pltpu.SMEM), whole(), whole()],
        out_specs=(whole(),) * (1 + len(DISTANCES)),
        compiler_params=vmem(12),
        name="pair",
    )(place, mine, other)
    return own, *(shift(block, "x", d, NX) for d, block in zip(DISTANCES, sent))


def per_device(
    crop_features, crop_counts, first_crop, tile_embed, dw_weight, conv_bias,
    ln_gain, ln_bias, w_up, b_up, w_down, b_down, gamma,
):
    f32 = jnp.float32
    width = b_down.shape[0]
    side = crop_features.shape[1]
    seq_index = lax.axis_index(SEQ)
    start = lax.axis_index(TP) * width
    blocks = gather_y(gather_z(w_up, w_down))

    def channels(array):
        return lax.dynamic_slice_in_dim(array, start, width, array.ndim - 1)

    slots = channels(crop_features)
    before, after = exchange(slots, seq_index, first_crop)
    table = channels(jnp.concatenate([dw_weight, tile_embed, conv_bias[None, :]]))
    block_in, conv = depthwise(
        seq_index, first_crop, crop_counts, slots, before, after, table
    )
    cells = PER_DEV * side * side
    padding = -cells % 128
    conv_t = jnp.pad(conv[:, :, :side].reshape(cells, width), ((0, padding), (0, 0))).T
    conv_t = conv_t.astype(jnp.float16)
    conv_all = lax.all_gather(conv_t, TP, axis=0, tiled=True).astype(f32)
    normed = layer_norm(conv_all, ln_gain, ln_bias)
    sums = mlp_sum(normed, blocks, b_up, width)
    result = pl.pallas_call(
        last_kernel,
        out_shape=jax.ShapeDtypeStruct((cells, width), jnp.bfloat16),
        in_specs=[whole()] * (len(sums) + 3),
        out_specs=whole(),
        compiler_params=vmem(12),
        name="result",
    )(*sums, b_down.astype(f32)[:, None], gamma[:, None], block_in.reshape(cells, width))
    return result.reshape(PER_DEV, side, side, width)


def solution(mesh):
    fine = Mesh(mesh.devices.reshape(NY, NZ, NX, NCORE), SEQ + TP)
    placed = (
        P(SEQ, None, None, None), P(), P(), P(), P(), P(), P(), P(),
        P(SEQ, TP), P(TP), P(TP, SEQ), P(TP), P(TP),
    )
    return jax.shard_map(
        per_device,
        mesh=fine,
        in_specs=placed,
        out_specs=P(SEQ, None, None, TP),
        check_vma=False,
    )
```

```python
import jax
import jax.numpy as jnp
from jax import lax
from jax.experimental import pallas as pl
from jax.experimental.pallas import tpu as pltpu
from jax.sharding import Mesh, PartitionSpec as P

NY, NZ, NX, NCORE = 4, 16, 4, 2
SEQ = ("y", "z")
TP = ("x", "core")
PER_DEV = 2
KSIDE = 7
DISTANCES = (2, 1, 3)


def shift(block, axis, distance, size):
    return lax.ppermute(block, axis, [(i, (i + distance) % size) for i in range(size)])


def gather_z(w_up, w_down):
    both = jnp.stack([w_up, w_down.T]).astype(jnp.float32) * 2.0**18
    over_z = lax.all_gather(both.astype(jnp.float16), "z", axis=1, tiled=True)
    return (over_z.astype(jnp.float32) * 2.0**-18).astype(jnp.bfloat16)


def gather_y(own):
    return own, *(shift(own, "y", -d, NY) for d in (1, 2, 3))


def exchange(slots, seq_index, first_crop):
    count = NY * NZ
    first = first_crop[seq_index]
    last_slot = slots.shape[0] - 1

    def crop(number):
        return lax.dynamic_index_in_dim(
            slots, jnp.clip(number - first, 0, last_slot), 0, keepdims=False
        )

    target = PER_DEV * seq_index
    before = lax.ppermute(
        crop(target + PER_DEV), SEQ, [(i, i + 1) for i in range(count - 1)]
    )
    after = lax.ppermute(crop(target - 1), SEQ, [(i + 1, i) for i in range(count - 1)])
    return before, after


def conv_kernel(
    seq, first_crop, crop_counts, slots, before, after, table,
    block_in, conv, padded, shifted, taps, rows, flat,
):
    f32 = jnp.float32
    side = rows.shape[1]
    cells = side * side
    shards = first_crop.shape[0]
    margin = KSIDE // 2
    here = seq[0]
    first = first_crop[here]
    limit = jnp.where(
        here + 1 < shards, first_crop[jnp.minimum(here + 1, shards - 1)], PER_DEV * shards
    )
    tile_at = KSIDE * KSIDE
    bias = table[tile_at + 3 : tile_at + 4, :].astype(f32)
    for t in range(KSIDE * KSIDE):
        taps[t] = jnp.broadcast_to(table[t : t + 1, :].astype(f32), taps.shape[1:])
    padded[...] = jnp.zeros_like(padded)
    shifted[...] = jnp.zeros_like(shifted)
    for n in range(PER_DEV):
        target = PER_DEV * here + n

        def image(i, carry):
            start, begin = carry
            return start + crop_counts[i], jnp.where(start <= target, start, begin)

        _, begin = lax.fori_loop(0, crop_counts.shape[0], image, (jnp.int32(0), jnp.int32(0)))
        place = target - begin
        tile = jnp.zeros_like(bias)
        for p in range(3):
            row = table[tile_at + p : tile_at + p + 1, :].astype(f32)
            tile = jnp.where(place == p, row, tile)
        mine = slots[jnp.clip(target - first, 0, slots.shape[0] - 1)].astype(f32)
        received = (before if n == 0 else after)[...].astype(f32)
        held = (first <= target) & (target < limit)
        crop = jnp.where(held, mine, received) + tile
        for i in range(side):
            at = n * cells + i * side
            block_in[at : at + side, :] = crop[i]
        padded[:, margin : margin + side, :] = crop
        for b in range(KSIDE):
            shifted[b, n, margin : margin + side] = padded[:, b : b + shifted.shape[3], :]
    columns, width = shifted.shape[3:]
    groups = side // 3

    def three_rows(g, _):
        n, top = lax.div(g, groups), lax.rem(g, groups) * 3
        sums = [jnp.zeros((columns // 8, 8, width), f32) for _ in range(3)]
        for b in range(KSIDE):
            for r in range(KSIDE + 2):
                row = shifted[b, n, top + r].reshape(columns // 8, 8, width)
                for o in range(3):
                    if 0 <= r - o < KSIDE:
                        sums[o] = sums[o] + row * taps[(r - o) * KSIDE + b][None]
        for o in range(3):
            rows[n, top + o] = sums[o].reshape(columns, width) + bias
        return 0

    lax.fori_loop(0, PER_DEV * groups, three_rows, 0)
    last = PER_DEV * cells // 8 * 8
    flat[last:, :] = jnp.zeros((flat.shape[0] - last, width), f32)
    for n in range(PER_DEV):
        for i in range(side):
            at = n * cells + i * side
            flat[at : at + side, :] = rows[n, i][:side]
    conv[...] = flat[...].T


def depthwise(seq_index, first_crop, crop_counts, slots, before, after, table):
    f32 = jnp.float32
    side, width = slots.shape[1], slots.shape[3]
    columns = 24
    cells = PER_DEV * side * side
    padded_cells = cells + -cells % 128
    return pl.pallas_call(
        conv_kernel,
        out_shape=(
            jax.ShapeDtypeStruct((cells, width), f32),
            jax.ShapeDtypeStruct((width, padded_cells), f32),
        ),
        in_specs=[whole(pltpu.SMEM)] * 3 + [whole()] * 4,
        out_specs=(whole(), whole()),
        scratch_shapes=[
            pltpu.VMEM((side, columns + 8, width), f32),
            pltpu.VMEM((KSIDE, PER_DEV, side + 6, columns, width), f32),
            pltpu.VMEM((KSIDE * KSIDE, 8, width), f32),
            pltpu.VMEM((PER_DEV, side, columns, width), f32),
            pltpu.VMEM((padded_cells, width), f32),
        ],
        compiler_params=vmem(18),
        name="conv",
    )(seq_index.astype(jnp.int32).reshape(1), first_crop, crop_counts, slots, before, after, table)


def vmem(mebibytes):
    return pltpu.CompilerParams(vmem_limit_bytes=mebibytes * 2**20)


def whole(space=pltpu.VMEM):
    return pl.BlockSpec(memory_space=space)


def norm_kernel(conv, gain_ref, bias_ref, normed):
    channels, cells = conv.shape
    gain = gain_ref[...].astype(jnp.float32)[None, :]
    bias = bias_ref[...].astype(jnp.float32)[None, :]
    step = 128
    for c in range(0, cells, step):
        block = conv[:, c : c + step]
        mean = jnp.sum(block, axis=0, keepdims=True) * (1.0 / channels)
        block = block - mean
        var = jnp.sum(block * block, axis=0, keepdims=True) * (1.0 / channels)
        block = block * lax.rsqrt(var + 1e-6)
        normed[c : c + step, :] = (block.T * gain + bias).astype(normed.dtype)


def layer_norm(conv, gain, bias):
    return pl.pallas_call(
        norm_kernel,
        out_shape=jax.ShapeDtypeStruct(conv.shape[::-1], jnp.bfloat16),
        in_specs=[whole()] * 3,
        out_specs=whole(),
        compiler_params=vmem(20),
        name="norm",
    )(conv, gain, bias)


def copy_down_rows(blocks, buffer, sems, y, core):
    width = buffer.shape[0] // NX
    copies = []
    for d, block in enumerate(blocks):
        source = pl.multiple_of(core * width, width)
        target = pl.multiple_of(lax.rem(y + d, NY) * width, width)
        copies.append(
            pltpu.make_async_copy(
                block.at[1, pl.ds(source, width), :], buffer.at[pl.ds(target, width), :], sems.at[d]
            )
        )
    return copies


def down_product(buffer, hidden, out):
    width = buffer.shape[0] // NX
    product = lax.dot_general(
        buffer[...], hidden, (((1,), (1,)), ((), ())), preferred_element_type=jnp.float32
    )
    for x in range(NX):
        out[x] = product[x * width : (x + 1) * width].astype(out.dtype)


def first_kernel(y_ref, core_ref, normed, b_up, *refs):
    blocks, (hidden, out, up, down, up_sem, down_sem) = refs[:NY], refs[NY:]
    y, core = y_ref[0], core_ref[0]
    bias = b_up[...].astype(jnp.float32)[None, :]
    ups = []
    for d, block in enumerate(blocks):
        rows = block.shape[1]
        target = pl.multiple_of(lax.rem(y + d, NY) * rows, rows)
        ups.append(pltpu.make_async_copy(block.at[0], up.at[pl.ds(target, rows), :], up_sem.at[d]))
    for copy in ups:
        copy.start()
    downs = copy_down_rows(blocks, down, down_sem, y, 1 - core)
    for copy in downs:
        copy.start()
    for copy in ups:
        copy.wait()
    cells, units = normed.shape[0], b_up.shape[0]
    rows = cells // 4
    for r in range(0, cells, rows):
        pre = jnp.dot(normed[r : r + rows], up[...], preferred_element_type=jnp.float32)
        pre = pre + bias
        act = 0.5 * pre * (1.0 + lax.erf(pre * 0.5**0.5))
        hidden[r : r + rows] = act.astype(hidden.dtype)
    for copy in downs:
        copy.wait()
    down_product(down, hidden[...], out)


def second_kernel(y, core, hidden, *refs):
    blocks, (out, down, down_sem) = refs[:NY], refs[NY:]
    downs = copy_down_rows(blocks, down, down_sem, y[0], core[0])
    for copy in downs:
        copy.start()
    for copy in downs:
        copy.wait()
    down_product(down, hidden[...], out)


def pair_kernel(x, mine, other, own, *sent):
    def pair(distance):
        i = lax.rem(x[0] + distance, NX)
        return mine[i].astype(jnp.float32) + other[i].astype(jnp.float32)

    own[...] = pair(0)
    for distance, block in zip(DISTANCES, sent):
        block[...] = pair(distance).astype(block.dtype)


def last_kernel(own, first, second, third, b_down, gamma, residual, out):
    total = own[...]
    for block in (first, second, third):
        total = total + block[...].astype(jnp.float32)
    scaled = gamma[...] * (total + b_down[...])
    rows = residual.shape[0]
    out[...] = (residual[...] + scaled.T[:rows]).astype(out.dtype)


def mlp_sum(normed, blocks, b_up, width):
    bf16, f32 = jnp.bfloat16, jnp.float32
    cells, units = normed.shape[0], b_up.shape[0]
    y, x, core = (lax.axis_index(a).astype(jnp.int32).reshape(1) for a in ("y", "x", "core"))
    half_out = jax.ShapeDtypeStruct((NX, width, cells), bf16)
    down = pltpu.VMEM((NX * width, units), bf16)
    hidden, other = pl.pallas_call(
        first_kernel,
        out_shape=(jax.ShapeDtypeStruct((cells, units), bf16), half_out),
        in_specs=[whole(pltpu.SMEM)] * 2 + [whole()] * 2 + [whole(pl.ANY)] * len(blocks),
        out_specs=(whole(), whole()),
        scratch_shapes=[
            pltpu.VMEM((normed.shape[1], units), bf16),
            down,
            pltpu.SemaphoreType.DMA((4,)),
            pltpu.SemaphoreType.DMA((NX,)),
        ],
        compiler_params=vmem(20),
        name="up_and_down",
    )(y, core, normed, b_up, *blocks)
    other = shift(other, "core", 1, NCORE)
    mine = pl.pallas_call(
        second_kernel,
        out_shape=half_out,
        in_specs=[whole(pltpu.SMEM)] * 2 + [whole()] + [whole(pl.ANY)] * len(blocks),
        out_specs=whole(),
        scratch_shapes=[down, pltpu.SemaphoreType.DMA((NX,))],
        compiler_params=vmem(12),
        name="down_own",
    )(y, core, hidden, *blocks)
    block = jax.ShapeDtypeStruct((width, cells), bf16)
    own, *sent = pl.pallas_call(
        pair_kernel,
        out_shape=(jax.ShapeDtypeStruct((width, cells), f32),) + (block,) * len(DISTANCES),
        in_specs=[whole(pltpu.SMEM), whole(), whole()],
        out_specs=(whole(),) * (1 + len(DISTANCES)),
        compiler_params=vmem(12),
        name="pair",
    )(x, mine, other)
    received = (shift(block, "x", d, NX) for d, block in zip(DISTANCES, sent))
    return own, *(pltpu.with_memory_space_constraint(r, pltpu.VMEM) for r in received)


def per_device(
    crop_features, crop_counts, first_crop, tile_embed, dw_weight, conv_bias,
    ln_gain, ln_bias, w_up, b_up, w_down, b_down, gamma,
):
    f32 = jnp.float32
    width = b_down.shape[0]
    side = crop_features.shape[1]
    seq_index = lax.axis_index(SEQ)
    start = lax.axis_index(TP) * width
    blocks = gather_y(gather_z(w_up, w_down))

    def channels(array):
        return lax.dynamic_slice_in_dim(array, start, width, array.ndim - 1)

    slots = channels(crop_features)
    before, after = exchange(slots, seq_index, first_crop)
    table = channels(jnp.concatenate([dw_weight, tile_embed, conv_bias[None, :]]))
    block_in, conv = depthwise(
        seq_index, first_crop, crop_counts, slots, before, after, table
    )
    cells = PER_DEV * side * side
    conv_t = conv.astype(jnp.float16)
    conv_all = lax.all_gather(conv_t, TP, axis=0, tiled=True).astype(f32)
    normed = layer_norm(conv_all, ln_gain, ln_bias)
    sums = mlp_sum(normed, blocks, b_up, width)
    result = pl.pallas_call(
        last_kernel,
        out_shape=jax.ShapeDtypeStruct((cells, width), jnp.bfloat16),
        in_specs=[whole()] * (len(sums) + 3),
        out_specs=whole(),
        compiler_params=vmem(12),
        name="result",
    )(*sums, b_down.astype(f32)[:, None], gamma[:, None], block_in)
    return result.reshape(PER_DEV, side, side, width)


def solution(mesh):
    fine = Mesh(mesh.devices.reshape(NY, NZ, NX, NCORE), SEQ + TP)
    placed = (
        P(SEQ, None, None, None), P(), P(), P(), P(), P(), P(), P(),
        P(SEQ, TP), P(TP), P(TP, SEQ), P(TP), P(TP),
    )
    return jax.shard_map(
        per_device,
        mesh=fine,
        in_specs=placed,
        out_specs=P(SEQ, None, None, TP),
        check_vma=False,
    )
```

```python
import jax
import jax.numpy as jnp
from jax import lax
from jax.experimental import pallas as pl
from jax.experimental.pallas import tpu as pltpu
from jax.sharding import Mesh, PartitionSpec as P

NY, NZ, NX, NCORE = 4, 16, 4, 2
PARITIES = 2
Z = ("z_half", "parity")
SEQ = ("y",) + Z
TP = ("x", "core")
PER_DEV = 2
KSIDE = 7
DISTANCES = (2, 1, 3)


def shift(block, axis, distance, size):
    return lax.ppermute(block, axis, [(i, (i + distance) % size) for i in range(size)])


def gather_own(w_up, w_down):
    both = jnp.stack([w_up, w_down.T])
    own = lax.all_gather(both, "z_half", axis=1, tiled=True)
    blocks = [own] + [shift(own, "y", -d, NY) for d in (1, 2, 3)]
    return jnp.stack([b[0] for b in blocks]), jnp.stack([b[1] for b in blocks])


def exchange(slots, seq_index, first_crop):
    count = NY * NZ
    first = first_crop[seq_index]
    last_slot = slots.shape[0] - 1

    def crop(number):
        return lax.dynamic_index_in_dim(
            slots, jnp.clip(number - first, 0, last_slot), 0, keepdims=False
        )

    target = PER_DEV * seq_index
    before = lax.ppermute(
        crop(target + PER_DEV), SEQ, [(i, i + 1) for i in range(count - 1)]
    )
    after = lax.ppermute(crop(target - 1), SEQ, [(i + 1, i) for i in range(count - 1)])
    return before, after


def conv_kernel(
    seq, first_crop, crop_counts, slots, before, after, table,
    block_in, conv, padded, shifted, taps, rows, flat,
):
    f32 = jnp.float32
    side = rows.shape[1]
    cells = side * side
    shards = first_crop.shape[0]
    margin = KSIDE // 2
    here = seq[0]
    first = first_crop[here]
    limit = jnp.where(
        here + 1 < shards, first_crop[jnp.minimum(here + 1, shards - 1)], PER_DEV * shards
    )
    tile_at = KSIDE * KSIDE
    bias = table[tile_at + 3 : tile_at + 4, :].astype(f32)
    for t in range(KSIDE * KSIDE):
        taps[t] = jnp.broadcast_to(table[t : t + 1, :].astype(f32), taps.shape[1:])
    padded[...] = jnp.zeros_like(padded)
    shifted[...] = jnp.zeros_like(shifted)
    for n in range(PER_DEV):
        target = PER_DEV * here + n

        def image(i, carry):
            start, begin = carry
            return start + crop_counts[i], jnp.where(start <= target, start, begin)

        _, begin = lax.fori_loop(0, crop_counts.shape[0], image, (jnp.int32(0), jnp.int32(0)))
        place = target - begin
        tile = jnp.zeros_like(bias)
        for p in range(3):
            row = table[tile_at + p : tile_at + p + 1, :].astype(f32)
            tile = jnp.where(place == p, row, tile)
        mine = slots[jnp.clip(target - first, 0, slots.shape[0] - 1)].astype(f32)
        received = (before if n == 0 else after)[...].astype(f32)
        held = (first <= target) & (target < limit)
        crop = jnp.where(held, mine, received) + tile
        for i in range(side):
            at = n * cells + i * side
            block_in[at : at + side, :] = crop[i]
        padded[:, margin : margin + side, :] = crop
        for b in range(KSIDE):
            shifted[b, n, margin : margin + side] = padded[:, b : b + shifted.shape[3], :]
    columns, width = shifted.shape[3:]
    groups = side // 3

    def three_rows(g, _):
        n, top = lax.div(g, groups), lax.rem(g, groups) * 3
        sums = [jnp.zeros((columns // 8, 8, width), f32) for _ in range(3)]
        for b in range(KSIDE):
            for r in range(KSIDE + 2):
                row = shifted[b, n, top + r].reshape(columns // 8, 8, width)
                for o in range(3):
                    if 0 <= r - o < KSIDE:
                        sums[o] = sums[o] + row * taps[(r - o) * KSIDE + b][None]
        for o in range(3):
            rows[n, top + o] = sums[o].reshape(columns, width) + bias
        return 0

    lax.fori_loop(0, PER_DEV * groups, three_rows, 0)
    last = PER_DEV * cells // 8 * 8
    flat[last:, :] = jnp.zeros((flat.shape[0] - last, width), f32)
    for n in range(PER_DEV):
        for i in range(side):
            at = n * cells + i * side
            flat[at : at + side, :] = rows[n, i][:side]
    conv[...] = flat[...].T


def depthwise(seq_index, first_crop, crop_counts, slots, before, after, table):
    f32 = jnp.float32
    side, width = slots.shape[1], slots.shape[3]
    columns = 24
    cells = PER_DEV * side * side
    padded_cells = cells + -cells % 128
    return pl.pallas_call(
        conv_kernel,
        out_shape=(
            jax.ShapeDtypeStruct((cells, width), f32),
            jax.ShapeDtypeStruct((width, padded_cells), f32),
        ),
        in_specs=[whole(pltpu.SMEM)] * 3 + [whole()] * 4,
        out_specs=(whole(), whole()),
        scratch_shapes=[
            pltpu.VMEM((side, columns + 8, width), f32),
            pltpu.VMEM((KSIDE, PER_DEV, side + 6, columns, width), f32),
            pltpu.VMEM((KSIDE * KSIDE, 8, width), f32),
            pltpu.VMEM((PER_DEV, side, columns, width), f32),
            pltpu.VMEM((padded_cells, width), f32),
        ],
        compiler_params=vmem(18),
        name="conv",
    )(seq_index.astype(jnp.int32).reshape(1), first_crop, crop_counts, slots, before, after, table)


def vmem(mebibytes):
    return pltpu.CompilerParams(vmem_limit_bytes=mebibytes * 2**20)


def whole(space=pltpu.VMEM):
    return pl.BlockSpec(memory_space=space)


def norm_kernel(conv, gain_ref, bias_ref, normed):
    channels, cells = conv.shape
    step = 128
    rows = channels // (NY * NZ)

    def columns(ref):
        line = ref[...].astype(jnp.float32)[None, :]
        return jnp.broadcast_to(line, (step, channels)).T

    gain, bias = columns(gain_ref), columns(bias_ref)
    order = [
        (y * NZ + z) * rows for p in range(PARITIES) for y in range(NY) for z in range(p, NZ, PARITIES)
    ]
    for c in range(0, cells, step):
        block = conv[:, c : c + step]
        mean = jnp.sum(block, axis=0, keepdims=True) * (1.0 / channels)
        block = block - mean
        var = jnp.sum(block * block, axis=0, keepdims=True) * (1.0 / channels)
        block = block * lax.rsqrt(var + 1e-6) * gain + bias
        block = jnp.concatenate([block[r : r + rows] for r in order])
        normed[c : c + step, :] = block.T.astype(normed.dtype)


def layer_norm(conv, gain, bias):
    return pl.pallas_call(
        norm_kernel,
        out_shape=jax.ShapeDtypeStruct(conv.shape[::-1], jnp.bfloat16),
        in_specs=[whole()] * 3,
        out_specs=whole(),
        compiler_params=vmem(20),
        name="norm",
    )(conv, gain, bias)


def copy_down_rows(near, far, buffer, sems, y, parity, core):
    width = buffer.shape[0] // NX
    half = width // PARITIES
    source = pl.multiple_of(core * half, half)
    copies = []
    for d in range(NY):
        start = lax.rem(y + d, NY) * width
        for blocks, of in ((near, parity), (far, 1 - parity)):
            target = pl.multiple_of(start + of * half, half)
            copies.append(
                pltpu.make_async_copy(
                    blocks.at[d, pl.ds(source, half), :],
                    buffer.at[pl.ds(target, half), :],
                    sems.at[len(copies)],
                )
            )
    return copies


def down_product(buffer, hidden, out):
    width = buffer.shape[0] // NX
    product = lax.dot_general(
        buffer[...], hidden, (((1,), (1,)), ((), ())), preferred_element_type=jnp.float32
    )
    for x in range(NX):
        out[x] = product[x * width : (x + 1) * width].astype(out.dtype)


def first_kernel(
    place, normed, b_up, near_up, far_up, near_down, far_down,
    hidden, out, up, down, up_sem, down_sem,
):
    y, parity, core = place[0], place[1], place[2]
    bias = b_up[...].astype(jnp.float32)[None, :]
    rows = near_up.shape[1]
    ups = []
    for d in range(NY):
        start = lax.rem(y + d, NY) * rows
        for blocks, of in ((near_up, parity), (far_up, 1 - parity)):
            target = pl.multiple_of(start + of * NY * rows, rows)
            ups.append(
                pltpu.make_async_copy(
                    blocks.at[d], up.at[pl.ds(target, rows), :], up_sem.at[len(ups)]
                )
            )
    for copy in ups:
        copy.start()
    downs = copy_down_rows(near_down, far_down, down, down_sem, y, parity, 1 - core)
    for copy in downs:
        copy.start()
    for copy in ups:
        copy.wait()
    cells, units = normed.shape[0], b_up.shape[0]
    rows = cells // 4
    for r in range(0, cells, rows):
        pre = jnp.dot(normed[r : r + rows], up[...], preferred_element_type=jnp.float32)
        pre = pre + bias
        act = 0.5 * pre * (1.0 + lax.erf(pre * 0.5**0.5))
        hidden[r : r + rows] = act.astype(hidden.dtype)
    for copy in downs:
        copy.wait()
    down_product(down, hidden[...], out)


def second_kernel(place, hidden, near_down, far_down, out, down, down_sem):
    downs = copy_down_rows(near_down, far_down, down, down_sem, place[0], place[1], place[2])
    for copy in downs:
        copy.start()
    for copy in downs:
        copy.wait()
    down_product(down, hidden[...], out)


def pair_kernel(x, mine, other, own, *sent):
    def pair(distance):
        i = lax.rem(x[0] + distance, NX)
        return mine[i].astype(jnp.float32) + other[i].astype(jnp.float32)

    own[...] = pair(0)
    for distance, block in zip(DISTANCES, sent):
        block[...] = pair(distance).astype(block.dtype)


def last_kernel(own, first, second, third, b_down, gamma, residual, out):
    total = own[...]
    for block in (first, second, third):
        total = total + block[...].astype(jnp.float32)
    half = total.shape[0] // PARITIES
    step = half // (NZ // PARITIES // NCORE)
    total = jnp.concatenate(
        [total[p * half + m : p * half + m + step] for m in range(0, half, step) for p in range(PARITIES)]
    )
    scaled = gamma[...] * (total + b_down[...])
    rows = residual.shape[0]
    out[...] = (residual[...] + scaled.T[:rows]).astype(out.dtype)


def mlp_sum(normed, blocks, b_up, width):
    bf16, f32 = jnp.bfloat16, jnp.float32
    cells, units = normed.shape[0], b_up.shape[0]
    axes = ("y", "parity", "core")
    place = jnp.stack([lax.axis_index(a).astype(jnp.int32) for a in axes])
    x = lax.axis_index("x").astype(jnp.int32).reshape(1)
    near_up, far_up, near_down, far_down = blocks
    half_out = jax.ShapeDtypeStruct((NX, width, cells), bf16)
    down = pltpu.VMEM((NX * width, units), bf16)
    hidden, other = pl.pallas_call(
        first_kernel,
        out_shape=(jax.ShapeDtypeStruct((cells, units), bf16), half_out),
        in_specs=[whole(pltpu.SMEM)] + [whole()] * 2 + [whole(pl.ANY)] * 4,
        out_specs=(whole(), whole()),
        scratch_shapes=[
            pltpu.VMEM((normed.shape[1], units), bf16),
            down,
            pltpu.SemaphoreType.DMA((NY * PARITIES,)),
            pltpu.SemaphoreType.DMA((NY * PARITIES,)),
        ],
        compiler_params=vmem(20),
        name="up_and_down",
    )(place, normed, b_up, *blocks)
    other = shift(other, "core", 1, NCORE)
    mine = pl.pallas_call(
        second_kernel,
        out_shape=half_out,
        in_specs=[whole(pltpu.SMEM), whole()] + [whole(pl.ANY)] * 2,
        out_specs=whole(),
        scratch_shapes=[down, pltpu.SemaphoreType.DMA((NY * PARITIES,))],
        compiler_params=vmem(12),
        name="down_own",
    )(place, hidden, near_down, far_down)
    block = jax.ShapeDtypeStruct((width, cells), bf16)
    own, *sent = pl.pallas_call(
        pair_kernel,
        out_shape=(jax.ShapeDtypeStruct((width, cells), f32),) + (block,) * len(DISTANCES),
        in_specs=[whole(pltpu.SMEM), whole(), whole()],
        out_specs=(whole(),) * (1 + len(DISTANCES)),
        compiler_params=vmem(12),
        name="pair",
    )(x, mine, other)
    received = (shift(block, "x", d, NX) for d, block in zip(DISTANCES, sent))
    return own, *(pltpu.with_memory_space_constraint(r, pltpu.VMEM) for r in received)


def per_device(
    crop_features, crop_counts, first_crop, tile_embed, dw_weight, conv_bias,
    ln_gain, ln_bias, w_up, b_up, w_down, b_down, gamma,
):
    f32 = jnp.float32
    width = b_down.shape[0]
    side = crop_features.shape[1]
    seq_index = lax.axis_index(SEQ)
    start = lax.axis_index(TP) * width
    near_up, near_down = gather_own(w_up, w_down)

    def channels(array):
        return lax.dynamic_slice_in_dim(array, start, width, array.ndim - 1)

    slots = channels(crop_features)
    before, after = exchange(slots, seq_index, first_crop)
    table = channels(jnp.concatenate([dw_weight, tile_embed, conv_bias[None, :]]))
    block_in, conv = depthwise(
        seq_index, first_crop, crop_counts, slots, before, after, table
    )
    cells = PER_DEV * side * side
    conv_t, near_up, near_down = lax.optimization_barrier(
        (conv.astype(jnp.float16), near_up, near_down)
    )
    blocks = (near_up, shift(near_up, Z, -1, NZ), near_down, shift(near_down, Z, 1, NZ))
    conv_all = lax.all_gather(conv_t, TP, axis=0, tiled=True).astype(f32)
    normed = layer_norm(conv_all, ln_gain, ln_bias)
    sums = mlp_sum(normed, blocks, b_up, width)
    result = pl.pallas_call(
        last_kernel,
        out_shape=jax.ShapeDtypeStruct((cells, width), jnp.bfloat16),
        in_specs=[whole()] * (len(sums) + 3),
        out_specs=whole(),
        compiler_params=vmem(12),
        name="result",
    )(*sums, b_down.astype(f32)[:, None], gamma[:, None], block_in)
    return result.reshape(PER_DEV, side, side, width)


def solution(mesh):
    fine = Mesh(mesh.devices.reshape(NY, NZ // PARITIES, PARITIES, NX, NCORE), SEQ + TP)
    placed = (
        P(SEQ, None, None, None), P(), P(), P(), P(), P(), P(), P(),
        P(SEQ, TP), P(TP), P(TP, SEQ), P(TP), P(TP),
    )
    return jax.shard_map(
        per_device,
        mesh=fine,
        in_specs=placed,
        out_specs=P(SEQ, None, None, TP),
        check_vma=False,
    )
```

```python
import jax
import jax.numpy as jnp
from jax import lax
from jax.experimental import pallas as pl
from jax.experimental.pallas import tpu as pltpu
from jax.sharding import Mesh, PartitionSpec as P

NY, NZ, NX, NCORE = 4, 16, 4, 2
SEQ = ("y", "z")
TP = ("x", "core")
PER_DEV = 2
KSIDE = 7
DISTANCES = (2, 1, 3)


def shift(block, axis, distance, size):
    return lax.ppermute(block, axis, [(i, (i + distance) % size) for i in range(size)])


def gather_z(w_up, w_down):
    both = jnp.stack([w_up, w_down.T]).astype(jnp.float32) * 2.0**18
    over_z = lax.all_gather(both.astype(jnp.float16), "z", axis=1, tiled=True)
    return (over_z.astype(jnp.float32) * 2.0**-18).astype(jnp.bfloat16)


def gather_y(own):
    copies = jnp.broadcast_to(own[None], (NY,) + own.shape)
    return lax.all_to_all(copies, "y", split_axis=0, concat_axis=0, tiled=True)


def exchange(slots, seq_index, first_crop):
    count = NY * NZ
    first = first_crop[seq_index]
    last_slot = slots.shape[0] - 1

    def crop(number):
        return lax.dynamic_index_in_dim(
            slots, jnp.clip(number - first, 0, last_slot), 0, keepdims=False
        )

    target = PER_DEV * seq_index
    before = lax.ppermute(
        crop(target + PER_DEV), SEQ, [(i, i + 1) for i in range(count - 1)]
    )
    after = lax.ppermute(crop(target - 1), SEQ, [(i + 1, i) for i in range(count - 1)])
    return before, after


def conv_kernel(
    seq, first_crop, crop_counts, slots, before, after, table,
    block_in, conv, padded, shifted, taps, rows, flat,
):
    f32 = jnp.float32
    side = rows.shape[1]
    cells = side * side
    shards = first_crop.shape[0]
    margin = KSIDE // 2
    here = seq[0]
    first = first_crop[here]
    limit = jnp.where(
        here + 1 < shards, first_crop[jnp.minimum(here + 1, shards - 1)], PER_DEV * shards
    )
    tile_at = KSIDE * KSIDE
    bias = table[tile_at + 3 : tile_at + 4, :].astype(f32)
    for t in range(KSIDE * KSIDE):
        taps[t] = jnp.broadcast_to(table[t : t + 1, :].astype(f32), taps.shape[1:])
    padded[...] = jnp.zeros_like(padded)
    shifted[...] = jnp.zeros_like(shifted)
    for n in range(PER_DEV):
        target = PER_DEV * here + n

        def image(i, carry):
            start, begin = carry
            return start + crop_counts[i], jnp.where(start <= target, start, begin)

        _, begin = lax.fori_loop(0, crop_counts.shape[0], image, (jnp.int32(0), jnp.int32(0)))
        place = target - begin
        tile = jnp.zeros_like(bias)
        for p in range(3):
            row = table[tile_at + p : tile_at + p + 1, :].astype(f32)
            tile = jnp.where(place == p, row, tile)
        mine = slots[jnp.clip(target - first, 0, slots.shape[0] - 1)].astype(f32)
        received = (before if n == 0 else after)[...].astype(f32)
        held = (first <= target) & (target < limit)
        crop = jnp.where(held, mine, received) + tile
        for i in range(side):
            at = n * cells + i * side
            block_in[at : at + side, :] = crop[i]
        padded[:, margin : margin + side, :] = crop
        for b in range(KSIDE):
            shifted[b, n, margin : margin + side] = padded[:, b : b + shifted.shape[3], :]
    columns, width = shifted.shape[3:]
    groups = side // 3

    def three_rows(g, _):
        n, top = lax.div(g, groups), lax.rem(g, groups) * 3
        sums = [jnp.zeros((columns // 8, 8, width), f32) for _ in range(3)]
        for b in range(KSIDE):
            for r in range(KSIDE + 2):
                row = shifted[b, n, top + r].reshape(columns // 8, 8, width)
                for o in range(3):
                    if 0 <= r - o < KSIDE:
                        sums[o] = sums[o] + row * taps[(r - o) * KSIDE + b][None]
        for o in range(3):
            rows[n, top + o] = sums[o].reshape(columns, width) + bias
        return 0

    lax.fori_loop(0, PER_DEV * groups, three_rows, 0)
    last = PER_DEV * cells // 8 * 8
    flat[last:, :] = jnp.zeros((flat.shape[0] - last, width), f32)
    for n in range(PER_DEV):
        for i in range(side):
            at = n * cells + i * side
            flat[at : at + side, :] = rows[n, i][:side]
    conv[...] = flat[...].T


def depthwise(seq_index, first_crop, crop_counts, slots, before, after, table):
    f32 = jnp.float32
    side, width = slots.shape[1], slots.shape[3]
    columns = 24
    cells = PER_DEV * side * side
    padded_cells = cells + -cells % 128
    return pl.pallas_call(
        conv_kernel,
        out_shape=(
            jax.ShapeDtypeStruct((cells, width), f32),
            jax.ShapeDtypeStruct((width, padded_cells), f32),
        ),
        in_specs=[whole(pltpu.SMEM)] * 3 + [whole()] * 4,
        out_specs=(whole(), whole()),
        scratch_shapes=[
            pltpu.VMEM((side, columns + 8, width), f32),
            pltpu.VMEM((KSIDE, PER_DEV, side + 6, columns, width), f32),
            pltpu.VMEM((KSIDE * KSIDE, 8, width), f32),
            pltpu.VMEM((PER_DEV, side, columns, width), f32),
            pltpu.VMEM((padded_cells, width), f32),
        ],
        compiler_params=vmem(18),
        name="conv",
    )(seq_index.astype(jnp.int32).reshape(1), first_crop, crop_counts, slots, before, after, table)


def vmem(mebibytes):
    return pltpu.CompilerParams(vmem_limit_bytes=mebibytes * 2**20)


def whole(space=pltpu.VMEM):
    return pl.BlockSpec(memory_space=space)


def norm_kernel(conv, gain_ref, bias_ref, normed):
    channels, cells = conv.shape
    gain = gain_ref[...].astype(jnp.float32)[None, :]
    bias = bias_ref[...].astype(jnp.float32)[None, :]
    step = 128
    for c in range(0, cells, step):
        block = conv[:, c : c + step]
        mean = jnp.sum(block, axis=0, keepdims=True) * (1.0 / channels)
        block = block - mean
        var = jnp.sum(block * block, axis=0, keepdims=True) * (1.0 / channels)
        block = block * lax.rsqrt(var + 1e-6)
        normed[c : c + step, :] = (block.T * gain + bias).astype(normed.dtype)


def layer_norm(conv, gain, bias):
    return pl.pallas_call(
        norm_kernel,
        out_shape=jax.ShapeDtypeStruct(conv.shape[::-1], jnp.bfloat16),
        in_specs=[whole()] * 3,
        out_specs=whole(),
        compiler_params=vmem(20),
        name="norm",
    )(conv, gain, bias)


def copy_down_rows(blocks, buffer, sems, core):
    width = buffer.shape[0] // NX
    source = pl.multiple_of(core * width, width)
    return [
        pltpu.make_async_copy(
            blocks.at[d, 1, pl.ds(source, width), :],
            buffer.at[pl.ds(d * width, width), :],
            sems.at[d],
        )
        for d in range(NY)
    ]


def down_product(buffer, hidden, out):
    width = buffer.shape[0] // NX
    product = lax.dot_general(
        buffer[...], hidden, (((1,), (1,)), ((), ())), preferred_element_type=jnp.float32
    )
    for x in range(NX):
        out[x] = product[x * width : (x + 1) * width].astype(out.dtype)


def first_kernel(core, normed, b_up, blocks, hidden, out, up, down, up_sem, down_sem):
    bias = b_up[...].astype(jnp.float32)[None, :]
    rows = blocks.shape[2]
    ups = [
        pltpu.make_async_copy(blocks.at[d, 0], up.at[pl.ds(d * rows, rows), :], up_sem.at[d])
        for d in range(NY)
    ]
    for copy in ups:
        copy.start()
    downs = copy_down_rows(blocks, down, down_sem, 1 - core[0])
    for copy in downs:
        copy.start()
    for copy in ups:
        copy.wait()
    cells, units = normed.shape[0], b_up.shape[0]
    rows = cells // 4
    for r in range(0, cells, rows):
        pre = jnp.dot(normed[r : r + rows], up[...], preferred_element_type=jnp.float32)
        pre = pre + bias
        act = 0.5 * pre * (1.0 + lax.erf(pre * 0.5**0.5))
        hidden[r : r + rows] = act.astype(hidden.dtype)
    for copy in downs:
        copy.wait()
    down_product(down, hidden[...], out)


def second_kernel(core, hidden, blocks, out, down, down_sem):
    downs = copy_down_rows(blocks, down, down_sem, core[0])
    for copy in downs:
        copy.start()
    for copy in downs:
        copy.wait()
    down_product(down, hidden[...], out)


def pair_kernel(x, mine, other, own, *sent):
    def pair(distance):
        i = lax.rem(x[0] + distance, NX)
        return mine[i].astype(jnp.float32) + other[i].astype(jnp.float32)

    own[...] = pair(0)
    for distance, block in zip(DISTANCES, sent):
        block[...] = pair(distance).astype(block.dtype)


def last_kernel(own, first, second, third, b_down, gamma, residual, out):
    total = own[...]
    for block in (first, second, third):
        total = total + block[...].astype(jnp.float32)
    scaled = gamma[...] * (total + b_down[...])
    rows = residual.shape[0]
    out[...] = (residual[...] + scaled.T[:rows]).astype(out.dtype)


def mlp_sum(normed, blocks, b_up, width):
    bf16, f32 = jnp.bfloat16, jnp.float32
    cells, units = normed.shape[0], b_up.shape[0]
    x, core = (lax.axis_index(a).astype(jnp.int32).reshape(1) for a in TP)
    half_out = jax.ShapeDtypeStruct((NX, width, cells), bf16)
    down = pltpu.VMEM((NX * width, units), bf16)
    hidden, other = pl.pallas_call(
        first_kernel,
        out_shape=(jax.ShapeDtypeStruct((cells, units), bf16), half_out),
        in_specs=[whole(pltpu.SMEM), whole(), whole(), whole(pl.ANY)],
        out_specs=(whole(), whole()),
        scratch_shapes=[
            pltpu.VMEM((normed.shape[1], units), bf16),
            down,
            pltpu.SemaphoreType.DMA((4,)),
            pltpu.SemaphoreType.DMA((NX,)),
        ],
        compiler_params=vmem(20),
        name="up_and_down",
    )(core, normed, b_up, blocks)
    other = shift(other, "core", 1, NCORE)
    mine = pl.pallas_call(
        second_kernel,
        out_shape=half_out,
        in_specs=[whole(pltpu.SMEM), whole(), whole(pl.ANY)],
        out_specs=whole(),
        scratch_shapes=[down, pltpu.SemaphoreType.DMA((NX,))],
        compiler_params=vmem(12),
        name="down_own",
    )(core, hidden, blocks)
    block = jax.ShapeDtypeStruct((width, cells), bf16)
    own, *sent = pl.pallas_call(
        pair_kernel,
        out_shape=(jax.ShapeDtypeStruct((width, cells), f32),) + (block,) * len(DISTANCES),
        in_specs=[whole(pltpu.SMEM), whole(), whole()],
        out_specs=(whole(),) * (1 + len(DISTANCES)),
        compiler_params=vmem(12),
        name="pair",
    )(x, mine, other)
    received = (shift(block, "x", d, NX) for d, block in zip(DISTANCES, sent))
    return own, *(pltpu.with_memory_space_constraint(r, pltpu.VMEM) for r in received)


def per_device(
    crop_features, crop_counts, first_crop, tile_embed, dw_weight, conv_bias,
    ln_gain, ln_bias, w_up, b_up, w_down, b_down, gamma,
):
    f32 = jnp.float32
    width = b_down.shape[0]
    side = crop_features.shape[1]
    seq_index = lax.axis_index(SEQ)
    start = lax.axis_index(TP) * width
    blocks = gather_y(gather_z(w_up, w_down))

    def channels(array):
        return lax.dynamic_slice_in_dim(array, start, width, array.ndim - 1)

    slots = channels(crop_features)
    before, after = exchange(slots, seq_index, first_crop)
    table = channels(jnp.concatenate([dw_weight, tile_embed, conv_bias[None, :]]))
    block_in, conv = depthwise(
        seq_index, first_crop, crop_counts, slots, before, after, table
    )
    cells = PER_DEV * side * side
    conv_t = conv.astype(jnp.float16)
    conv_all = lax.all_gather(conv_t, TP, axis=0, tiled=True).astype(f32)
    normed = layer_norm(conv_all, ln_gain, ln_bias)
    sums = mlp_sum(normed, blocks, b_up, width)
    result = pl.pallas_call(
        last_kernel,
        out_shape=jax.ShapeDtypeStruct((cells, width), jnp.bfloat16),
        in_specs=[whole()] * (len(sums) + 3),
        out_specs=whole(),
        compiler_params=vmem(12),
        name="result",
    )(*sums, b_down.astype(f32)[:, None], gamma[:, None], block_in)
    return result.reshape(PER_DEV, side, side, width)


def solution(mesh):
    fine = Mesh(mesh.devices.reshape(NY, NZ, NX, NCORE), SEQ + TP)
    placed = (
        P(SEQ, None, None, None), P(), P(), P(), P(), P(), P(), P(),
        P(SEQ, TP), P(TP), P(TP, SEQ), P(TP), P(TP),
    )
    return jax.shard_map(
        per_device,
        mesh=fine,
        in_specs=placed,
        out_specs=P(SEQ, None, None, TP),
        check_vma=False,
    )
```

```python
import jax
import jax.numpy as jnp
from jax import lax
from jax.experimental import pallas as pl
from jax.experimental.pallas import tpu as pltpu
from jax.sharding import Mesh, PartitionSpec as P

NY, NZ, NX, NCORE = 4, 16, 4, 2
SEQ = ("y", "z")
TP = ("x", "core")
PER_DEV = 2
KSIDE = 7
DISTANCES = (2, 1, 3)
Y_STEPS = (0, 2, 1, 3)


def shift(block, axis, distance, size):
    return lax.ppermute(block, axis, [(i, (i + distance) % size) for i in range(size)])


def gather_z(w_up, w_down):
    both = jnp.stack([w_up, w_down.T]).astype(jnp.float32) * 2.0**18
    over_z = lax.all_gather(both.astype(jnp.float16), "z", axis=1, tiled=True)
    return (over_z.astype(jnp.float32) * 2.0**-18).astype(jnp.bfloat16)


def gather_y(own):
    return own, *(shift(own, "y", -d, NY) for d in Y_STEPS[1:])


def exchange(slots, seq_index, first_crop):
    count = NY * NZ
    first = first_crop[seq_index]
    last_slot = slots.shape[0] - 1

    def crop(number):
        return lax.dynamic_index_in_dim(
            slots, jnp.clip(number - first, 0, last_slot), 0, keepdims=False
        )

    target = PER_DEV * seq_index
    before = lax.ppermute(
        crop(target + PER_DEV), SEQ, [(i, i + 1) for i in range(count - 1)]
    )
    after = lax.ppermute(crop(target - 1), SEQ, [(i + 1, i) for i in range(count - 1)])
    return before, after


def conv_kernel(
    seq, first_crop, crop_counts, slots, before, after, table,
    block_in, conv, padded, shifted, taps, rows, flat,
):
    f32 = jnp.float32
    side = rows.shape[1]
    cells = side * side
    shards = first_crop.shape[0]
    margin = KSIDE // 2
    here = seq[0]
    first = first_crop[here]
    limit = jnp.where(
        here + 1 < shards, first_crop[jnp.minimum(here + 1, shards - 1)], PER_DEV * shards
    )
    tile_at = KSIDE * KSIDE
    bias = table[tile_at + 3 : tile_at + 4, :].astype(f32)
    for t in range(KSIDE * KSIDE):
        taps[t] = jnp.broadcast_to(table[t : t + 1, :].astype(f32), taps.shape[1:])
    padded[...] = jnp.zeros_like(padded)
    edge = jnp.zeros((KSIDE, PER_DEV, margin) + shifted.shape[3:], f32)
    shifted[:, :, :margin] = edge
    shifted[:, :, margin + side :] = edge
    for n in range(PER_DEV):
        target = PER_DEV * here + n

        def image(i, carry):
            start, begin = carry
            return start + crop_counts[i], jnp.where(start <= target, start, begin)

        _, begin = lax.fori_loop(0, crop_counts.shape[0], image, (jnp.int32(0), jnp.int32(0)))
        place = target - begin
        tile = jnp.zeros_like(bias)
        for p in range(3):
            row = table[tile_at + p : tile_at + p + 1, :].astype(f32)
            tile = jnp.where(place == p, row, tile)
        mine = slots[jnp.clip(target - first, 0, slots.shape[0] - 1)].astype(f32)
        received = (before if n == 0 else after)[...].astype(f32)
        held = (first <= target) & (target < limit)
        crop = jnp.where(held, mine, received) + tile
        for i in range(side):
            at = n * cells + i * side
            block_in[at : at + side, :] = crop[i]
        padded[:, margin : margin + side, :] = crop
        for b in range(KSIDE):
            shifted[b, n, margin : margin + side] = padded[:, b : b + shifted.shape[3], :]
    columns, width = shifted.shape[3:]
    groups = side // 3

    def three_rows(g, _):
        n, top = lax.div(g, groups), lax.rem(g, groups) * 3
        sums = [jnp.zeros((columns // 8, 8, width), f32) for _ in range(3)]
        for b in range(KSIDE):
            for r in range(KSIDE + 2):
                row = shifted[b, n, top + r].reshape(columns // 8, 8, width)
                for o in range(3):
                    if 0 <= r - o < KSIDE:
                        sums[o] = sums[o] + row * taps[(r - o) * KSIDE + b][None]
        for o in range(3):
            rows[n, top + o] = sums[o].reshape(columns, width) + bias
        return 0

    lax.fori_loop(0, PER_DEV * groups, three_rows, 0)
    last = PER_DEV * cells // 8 * 8
    flat[last:, :] = jnp.zeros((flat.shape[0] - last, width), f32)
    for n in range(PER_DEV):
        for i in range(side):
            at = n * cells + i * side
            flat[at : at + side, :] = rows[n, i][:side]
    conv[...] = flat[...].T


def depthwise(seq_index, first_crop, crop_counts, slots, before, after, table):
    f32 = jnp.float32
    side, width = slots.shape[1], slots.shape[3]
    columns = 24
    cells = PER_DEV * side * side
    padded_cells = cells + -cells % 128
    return pl.pallas_call(
        conv_kernel,
        out_shape=(
            jax.ShapeDtypeStruct((cells, width), f32),
            jax.ShapeDtypeStruct((width, padded_cells), f32),
        ),
        in_specs=[whole(pltpu.SMEM)] * 3 + [whole()] * 4,
        out_specs=(whole(), whole()),
        scratch_shapes=[
            pltpu.VMEM((side, columns + 8, width), f32),
            pltpu.VMEM((KSIDE, PER_DEV, side + 6, columns, width), f32),
            pltpu.VMEM((KSIDE * KSIDE, 8, width), f32),
            pltpu.VMEM((PER_DEV, side, columns, width), f32),
            pltpu.VMEM((padded_cells, width), f32),
        ],
        compiler_params=vmem(18),
        name="conv",
    )(seq_index.astype(jnp.int32).reshape(1), first_crop, crop_counts, slots, before, after, table)


def vmem(mebibytes):
    return pltpu.CompilerParams(vmem_limit_bytes=mebibytes * 2**20)


def whole(space=pltpu.VMEM):
    return pl.BlockSpec(memory_space=space)


def norm_kernel(conv, gain_ref, bias_ref, normed):
    channels, cells = conv.shape
    gain = gain_ref[...].astype(jnp.float32)[None, :]
    bias = bias_ref[...].astype(jnp.float32)[None, :]
    step = 128
    for c in range(0, cells, step):
        block = conv[:, c : c + step]
        mean = jnp.sum(block, axis=0, keepdims=True) * (1.0 / channels)
        block = block - mean
        var = jnp.sum(block * block, axis=0, keepdims=True) * (1.0 / channels)
        block = block * lax.rsqrt(var + 1e-6)
        normed[c : c + step, :] = (block.T * gain + bias).astype(normed.dtype)


def layer_norm(conv, gain, bias):
    return pl.pallas_call(
        norm_kernel,
        out_shape=jax.ShapeDtypeStruct(conv.shape[::-1], jnp.bfloat16),
        in_specs=[whole()] * 3,
        out_specs=whole(),
        compiler_params=vmem(20),
        name="norm",
    )(conv, gain, bias)


def copy_down_rows(blocks, buffer, sems, y, core):
    width = buffer.shape[0] // NX
    copies = []
    for d, block in zip(Y_STEPS, blocks):
        source = pl.multiple_of(core * width, width)
        target = pl.multiple_of(lax.rem(y + d, NY) * width, width)
        copies.append(
            pltpu.make_async_copy(
                block.at[1, pl.ds(source, width), :], buffer.at[pl.ds(target, width), :], sems.at[d]
            )
        )
    return copies


def down_product(buffer, hidden, out):
    width = buffer.shape[0] // NX
    product = lax.dot_general(
        buffer[...], hidden, (((1,), (1,)), ((), ())), preferred_element_type=jnp.float32
    )
    for x in range(NX):
        out[x] = product[x * width : (x + 1) * width].astype(out.dtype)


def first_kernel(y_ref, core_ref, normed, b_up, *refs):
    blocks, (hidden, out, up, down, up_sem, down_sem) = refs[:NY], refs[NY:]
    y, core = y_ref[0], core_ref[0]
    bias = b_up[...].astype(jnp.float32)[None, :]
    ups = []
    for d, block in zip(Y_STEPS, blocks):
        rows = block.shape[1]
        target = pl.multiple_of(lax.rem(y + d, NY) * rows, rows)
        ups.append(pltpu.make_async_copy(block.at[0], up.at[pl.ds(target, rows), :], up_sem.at[d]))
    for copy in ups:
        copy.start()
    downs = copy_down_rows(blocks, down, down_sem, y, 1 - core)
    for copy in downs:
        copy.start()
    for copy in ups:
        copy.wait()
    cells, units = normed.shape[0], b_up.shape[0]
    rows = cells // 4
    for r in range(0, cells, rows):
        pre = jnp.dot(normed[r : r + rows], up[...], preferred_element_type=jnp.float32)
        pre = pre + bias
        act = 0.5 * pre * (1.0 + lax.erf(pre * 0.5**0.5))
        hidden[r : r + rows] = act.astype(hidden.dtype)
    for copy in downs:
        copy.wait()
    down_product(down, hidden[...], out)


def second_kernel(y, core, hidden, *refs):
    blocks, (out, down, down_sem) = refs[:NY], refs[NY:]
    downs = copy_down_rows(blocks, down, down_sem, y[0], core[0])
    for copy in downs:
        copy.start()
    for copy in downs:
        copy.wait()
    down_product(down, hidden[...], out)


def pair_kernel(x, mine, other, own, *sent):
    def pair(distance):
        i = lax.rem(x[0] + distance, NX)
        return mine[i].astype(jnp.float32) + other[i].astype(jnp.float32)

    own[...] = pair(0)
    for distance, block in zip(DISTANCES, sent):
        block[...] = pair(distance).astype(block.dtype)


def last_kernel(own, first, second, third, b_down, gamma, residual, out):
    total = own[...]
    for block in (first, second, third):
        total = total + block[...].astype(jnp.float32)
    scaled = gamma[...] * (total + b_down[...])
    rows = residual.shape[0]
    out[...] = (residual[...] + scaled.T[:rows]).astype(out.dtype)


def mlp_sum(normed, blocks, b_up, width):
    bf16, f32 = jnp.bfloat16, jnp.float32
    cells, units = normed.shape[0], b_up.shape[0]
    y, x, core = (lax.axis_index(a).astype(jnp.int32).reshape(1) for a in ("y", "x", "core"))
    half_out = jax.ShapeDtypeStruct((NX, width, cells), bf16)
    down = pltpu.VMEM((NX * width, units), bf16)
    hidden, other = pl.pallas_call(
        first_kernel,
        out_shape=(jax.ShapeDtypeStruct((cells, units), bf16), half_out),
        in_specs=[whole(pltpu.SMEM)] * 2 + [whole()] * 2 + [whole(pl.ANY)] * len(blocks),
        out_specs=(whole(), whole()),
        scratch_shapes=[
            pltpu.VMEM((normed.shape[1], units), bf16),
            down,
            pltpu.SemaphoreType.DMA((4,)),
            pltpu.SemaphoreType.DMA((NX,)),
        ],
        compiler_params=vmem(20),
        name="up_and_down",
    )(y, core, normed, b_up, *blocks)
    other = shift(other, "core", 1, NCORE)
    mine = pl.pallas_call(
        second_kernel,
        out_shape=half_out,
        in_specs=[whole(pltpu.SMEM)] * 2 + [whole()] + [whole(pl.ANY)] * len(blocks),
        out_specs=whole(),
        scratch_shapes=[down, pltpu.SemaphoreType.DMA((NX,))],
        compiler_params=vmem(12),
        name="down_own",
    )(y, core, hidden, *blocks)
    block = jax.ShapeDtypeStruct((width, cells), bf16)
    own, *sent = pl.pallas_call(
        pair_kernel,
        out_shape=(jax.ShapeDtypeStruct((width, cells), f32),) + (block,) * len(DISTANCES),
        in_specs=[whole(pltpu.SMEM), whole(), whole()],
        out_specs=(whole(),) * (1 + len(DISTANCES)),
        compiler_params=vmem(12),
        name="pair",
    )(x, mine, other)
    received = (shift(block, "x", d, NX) for d, block in zip(DISTANCES, sent))
    return own, *(pltpu.with_memory_space_constraint(r, pltpu.VMEM) for r in received)


def per_device(
    crop_features, crop_counts, first_crop, tile_embed, dw_weight, conv_bias,
    ln_gain, ln_bias, w_up, b_up, w_down, b_down, gamma,
):
    f32 = jnp.float32
    width = b_down.shape[0]
    side = crop_features.shape[1]
    seq_index = lax.axis_index(SEQ)
    start = lax.axis_index(TP) * width
    blocks = gather_y(gather_z(w_up, w_down))

    def channels(array):
        return lax.dynamic_slice_in_dim(array, start, width, array.ndim - 1)

    slots = channels(crop_features)
    before, after = exchange(slots, seq_index, first_crop)
    table = channels(jnp.concatenate([dw_weight, tile_embed, conv_bias[None, :]]))
    block_in, conv = depthwise(
        seq_index, first_crop, crop_counts, slots, before, after, table
    )
    cells = PER_DEV * side * side
    conv_t = conv.astype(jnp.float16)
    conv_all = lax.all_gather(conv_t, TP, axis=0, tiled=True).astype(f32)
    normed = layer_norm(conv_all, ln_gain, ln_bias)
    sums = mlp_sum(normed, blocks, b_up, width)
    result = pl.pallas_call(
        last_kernel,
        out_shape=jax.ShapeDtypeStruct((cells, width), jnp.bfloat16),
        in_specs=[whole()] * (len(sums) + 3),
        out_specs=whole(),
        compiler_params=vmem(12),
        name="result",
    )(*sums, b_down.astype(f32)[:, None], gamma[:, None], block_in)
    return result.reshape(PER_DEV, side, side, width)


def solution(mesh):
    fine = Mesh(mesh.devices.reshape(NY, NZ, NX, NCORE), SEQ + TP)
    placed = (
        P(SEQ, None, None, None), P(), P(), P(), P(), P(), P(), P(),
        P(SEQ, TP), P(TP), P(TP, SEQ), P(TP), P(TP),
    )
    return jax.shard_map(
        per_device,
        mesh=fine,
        in_specs=placed,
        out_specs=P(SEQ, None, None, TP),
        check_vma=False,
    )
```

```python
import jax
import jax.numpy as jnp
from jax import lax
from jax.experimental import pallas as pl
from jax.experimental.pallas import tpu as pltpu
from jax.sharding import Mesh, PartitionSpec as P

NY, NZ, NX, NCORE = 4, 16, 4, 2
SEQ = ("y", "z")
TP = ("x", "core")
PER_DEV = 2
KSIDE = 7
DISTANCES = (2, 1, 3)
Y_STEPS = (0, 2, 1, 3)


def shift(block, axis, distance, size):
    return lax.ppermute(block, axis, [(i, (i + distance) % size) for i in range(size)])


def gather_z(w_up, w_down):
    both = jnp.stack([w_up, w_down.T]).astype(jnp.float32) * 2.0**18
    over_z = lax.all_gather(both.astype(jnp.float16), "z", axis=1, tiled=True)
    return (over_z.astype(jnp.float32) * 2.0**-18).astype(jnp.bfloat16)


def gather_y(own):
    return own, *(shift(own, "y", -d, NY) for d in Y_STEPS[1:])


def exchange(slots, seq_index, first_crop):
    count = NY * NZ
    first = first_crop[seq_index]
    last_slot = slots.shape[0] - 1

    def crop(number):
        return lax.dynamic_index_in_dim(
            slots, jnp.clip(number - first, 0, last_slot), 0, keepdims=False
        )

    target = PER_DEV * seq_index
    before = lax.ppermute(
        crop(target + PER_DEV), SEQ, [(i, i + 1) for i in range(count - 1)]
    )
    after = lax.ppermute(crop(target - 1), SEQ, [(i + 1, i) for i in range(count - 1)])
    return before, after


def conv_kernel(
    seq, first_crop, crop_counts, slots, before, after, table,
    block_out, conv, padded, shifted, taps, rows, flat, block_in, sem,
):
    f32 = jnp.float32
    side = rows.shape[1]
    cells = side * side
    shards = first_crop.shape[0]
    margin = KSIDE // 2
    here = seq[0]
    first = first_crop[here]
    limit = jnp.where(
        here + 1 < shards, first_crop[jnp.minimum(here + 1, shards - 1)], PER_DEV * shards
    )
    tile_at = KSIDE * KSIDE
    bias = table[tile_at + 3 : tile_at + 4, :].astype(f32)
    for t in range(KSIDE * KSIDE):
        taps[t] = jnp.broadcast_to(table[t : t + 1, :].astype(f32), taps.shape[1:])
    padded[...] = jnp.zeros_like(padded)
    edge = jnp.zeros((KSIDE, PER_DEV, margin) + shifted.shape[3:], f32)
    shifted[:, :, :margin] = edge
    shifted[:, :, margin + side :] = edge
    for n in range(PER_DEV):
        target = PER_DEV * here + n

        def image(i, carry):
            start, begin = carry
            return start + crop_counts[i], jnp.where(start <= target, start, begin)

        _, begin = lax.fori_loop(0, crop_counts.shape[0], image, (jnp.int32(0), jnp.int32(0)))
        place = target - begin
        tile = jnp.zeros_like(bias)
        for p in range(3):
            row = table[tile_at + p : tile_at + p + 1, :].astype(f32)
            tile = jnp.where(place == p, row, tile)
        mine = slots[jnp.clip(target - first, 0, slots.shape[0] - 1)].astype(f32)
        received = (before if n == 0 else after)[...].astype(f32)
        held = (first <= target) & (target < limit)
        crop = jnp.where(held, mine, received) + tile
        for i in range(side):
            at = n * cells + i * side
            block_in[at : at + side, :] = crop[i]
        padded[:, margin : margin + side, :] = crop
        for b in range(KSIDE):
            shifted[b, n, margin : margin + side] = padded[:, b : b + shifted.shape[3], :]
    keep = pltpu.make_async_copy(block_in, block_out, sem)
    keep.start()
    columns, width = shifted.shape[3:]
    groups = side // 3

    def three_rows(g, _):
        n, top = lax.div(g, groups), lax.rem(g, groups) * 3
        sums = [jnp.zeros((columns // 8, 8, width), f32) for _ in range(3)]
        for b in range(KSIDE):
            for r in range(KSIDE + 2):
                row = shifted[b, n, top + r].reshape(columns // 8, 8, width)
                for o in range(3):
                    if 0 <= r - o < KSIDE:
                        sums[o] = sums[o] + row * taps[(r - o) * KSIDE + b][None]
        for o in range(3):
            rows[n, top + o] = sums[o].reshape(columns, width) + bias
        return 0

    lax.fori_loop(0, PER_DEV * groups, three_rows, 0)
    last = PER_DEV * cells // 8 * 8
    flat[last:, :] = jnp.zeros((flat.shape[0] - last, width), f32)
    for n in range(PER_DEV):
        for i in range(side):
            at = n * cells + i * side
            flat[at : at + side, :] = rows[n, i][:side]
    conv[...] = flat[...].T
    keep.wait()


def depthwise(seq_index, first_crop, crop_counts, slots, before, after, table):
    f32 = jnp.float32
    side, width = slots.shape[1], slots.shape[3]
    columns = 24
    cells = PER_DEV * side * side
    padded_cells = cells + -cells % 128
    return pl.pallas_call(
        conv_kernel,
        out_shape=(
            pltpu.HBM((cells, width), f32),
            jax.ShapeDtypeStruct((width, padded_cells), f32),
        ),
        in_specs=[whole(pltpu.SMEM)] * 3 + [whole()] * 4,
        out_specs=(whole(pltpu.HBM), whole()),
        scratch_shapes=[
            pltpu.VMEM((side, columns + 8, width), f32),
            pltpu.VMEM((KSIDE, PER_DEV, side + 6, columns, width), f32),
            pltpu.VMEM((KSIDE * KSIDE, 8, width), f32),
            pltpu.VMEM((PER_DEV, side, columns, width), f32),
            pltpu.VMEM((padded_cells, width), f32),
            pltpu.VMEM((cells, width), f32),
            pltpu.SemaphoreType.DMA,
        ],
        compiler_params=vmem(18),
        name="conv",
    )(seq_index.astype(jnp.int32).reshape(1), first_crop, crop_counts, slots, before, after, table)


def vmem(mebibytes):
    return pltpu.CompilerParams(vmem_limit_bytes=mebibytes * 2**20)


def whole(space=pltpu.VMEM):
    return pl.BlockSpec(memory_space=space)


def norm_kernel(conv, gain_ref, bias_ref, normed):
    channels, cells = conv.shape
    gain = gain_ref[...].astype(jnp.float32)[None, :]
    bias = bias_ref[...].astype(jnp.float32)[None, :]
    step = 128
    for c in range(0, cells, step):
        block = conv[:, c : c + step]
        mean = jnp.sum(block, axis=0, keepdims=True) * (1.0 / channels)
        block = block - mean
        var = jnp.sum(block * block, axis=0, keepdims=True) * (1.0 / channels)
        block = block * lax.rsqrt(var + 1e-6)
        normed[c : c + step, :] = (block.T * gain + bias).astype(normed.dtype)


def layer_norm(conv, gain, bias):
    return pl.pallas_call(
        norm_kernel,
        out_shape=jax.ShapeDtypeStruct(conv.shape[::-1], jnp.bfloat16),
        in_specs=[whole()] * 3,
        out_specs=whole(),
        compiler_params=vmem(20),
        name="norm",
    )(conv, gain, bias)


def copy_down_rows(blocks, buffer, sems, y, core):
    width = buffer.shape[0] // NX
    copies = []
    for d, block in zip(Y_STEPS, blocks):
        source = pl.multiple_of(core * width, width)
        target = pl.multiple_of(lax.rem(y + d, NY) * width, width)
        copies.append(
            pltpu.make_async_copy(
                block.at[1, pl.ds(source, width), :], buffer.at[pl.ds(target, width), :], sems.at[d]
            )
        )
    return copies


def down_product(buffer, hidden, out):
    width = buffer.shape[0] // NX
    product = lax.dot_general(
        buffer[...], hidden, (((1,), (1,)), ((), ())), preferred_element_type=jnp.float32
    )
    for x in range(NX):
        out[x] = product[x * width : (x + 1) * width].astype(out.dtype)


def first_kernel(y_ref, core_ref, normed, b_up, *refs):
    blocks, (hidden, out, up, down, up_sem, down_sem) = refs[:NY], refs[NY:]
    y, core = y_ref[0], core_ref[0]
    bias = b_up[...].astype(jnp.float32)[None, :]
    ups = []
    for d, block in zip(Y_STEPS, blocks):
        rows = block.shape[1]
        target = pl.multiple_of(lax.rem(y + d, NY) * rows, rows)
        ups.append(pltpu.make_async_copy(block.at[0], up.at[pl.ds(target, rows), :], up_sem.at[d]))
    for copy in ups:
        copy.start()
    downs = copy_down_rows(blocks, down, down_sem, y, 1 - core)
    for copy in downs:
        copy.start()
    for copy in ups:
        copy.wait()
    cells, units = normed.shape[0], b_up.shape[0]
    rows = cells // 4
    for r in range(0, cells, rows):
        pre = jnp.dot(normed[r : r + rows], up[...], preferred_element_type=jnp.float32)
        pre = pre + bias
        act = 0.5 * pre * (1.0 + lax.erf(pre * 0.5**0.5))
        hidden[r : r + rows] = act.astype(hidden.dtype)
    for copy in downs:
        copy.wait()
    down_product(down, hidden[...], out)


def second_kernel(y, core, hidden, *refs):
    blocks, (out, down, down_sem) = refs[:NY], refs[NY:]
    downs = copy_down_rows(blocks, down, down_sem, y[0], core[0])
    for copy in downs:
        copy.start()
    for copy in downs:
        copy.wait()
    down_product(down, hidden[...], out)


def pair_kernel(x, mine, other, own, *sent):
    def pair(distance):
        i = lax.rem(x[0] + distance, NX)
        return mine[i].astype(jnp.float32) + other[i].astype(jnp.float32)

    own[...] = pair(0)
    for distance, block in zip(DISTANCES, sent):
        block[...] = pair(distance).astype(block.dtype)


def last_kernel(own, first, second, third, b_down, gamma, residual, out):
    total = own[...]
    for block in (first, second, third):
        total = total + block[...].astype(jnp.float32)
    scaled = gamma[...] * (total + b_down[...])
    rows = residual.shape[0]
    out[...] = (residual[...] + scaled.T[:rows]).astype(out.dtype)


def mlp_sum(normed, blocks, b_up, width):
    bf16, f32 = jnp.bfloat16, jnp.float32
    cells, units = normed.shape[0], b_up.shape[0]
    y, x, core = (lax.axis_index(a).astype(jnp.int32).reshape(1) for a in ("y", "x", "core"))
    half_out = jax.ShapeDtypeStruct((NX, width, cells), bf16)
    down = pltpu.VMEM((NX * width, units), bf16)
    hidden, other = pl.pallas_call(
        first_kernel,
        out_shape=(jax.ShapeDtypeStruct((cells, units), bf16), half_out),
        in_specs=[whole(pltpu.SMEM)] * 2 + [whole()] * 2 + [whole(pl.ANY)] * len(blocks),
        out_specs=(whole(), whole()),
        scratch_shapes=[
            pltpu.VMEM((normed.shape[1], units), bf16),
            down,
            pltpu.SemaphoreType.DMA((4,)),
            pltpu.SemaphoreType.DMA((NX,)),
        ],
        compiler_params=vmem(20),
        name="up_and_down",
    )(y, core, normed, b_up, *blocks)
    other = shift(other, "core", 1, NCORE)
    mine = pl.pallas_call(
        second_kernel,
        out_shape=half_out,
        in_specs=[whole(pltpu.SMEM)] * 2 + [whole()] + [whole(pl.ANY)] * len(blocks),
        out_specs=whole(),
        scratch_shapes=[down, pltpu.SemaphoreType.DMA((NX,))],
        compiler_params=vmem(12),
        name="down_own",
    )(y, core, hidden, *blocks)
    block = jax.ShapeDtypeStruct((width, cells), bf16)
    own, *sent = pl.pallas_call(
        pair_kernel,
        out_shape=(jax.ShapeDtypeStruct((width, cells), f32),) + (block,) * len(DISTANCES),
        in_specs=[whole(pltpu.SMEM), whole(), whole()],
        out_specs=(whole(),) * (1 + len(DISTANCES)),
        compiler_params=vmem(12),
        name="pair",
    )(x, mine, other)
    received = (shift(block, "x", d, NX) for d, block in zip(DISTANCES, sent))
    return own, *(pltpu.with_memory_space_constraint(r, pltpu.VMEM) for r in received)


def per_device(
    crop_features, crop_counts, first_crop, tile_embed, dw_weight, conv_bias,
    ln_gain, ln_bias, w_up, b_up, w_down, b_down, gamma,
):
    f32 = jnp.float32
    width = b_down.shape[0]
    side = crop_features.shape[1]
    seq_index = lax.axis_index(SEQ)
    start = lax.axis_index(TP) * width
    blocks = gather_y(gather_z(w_up, w_down))

    def channels(array):
        return lax.dynamic_slice_in_dim(array, start, width, array.ndim - 1)

    slots = channels(crop_features)
    before, after = exchange(slots, seq_index, first_crop)
    table = channels(jnp.concatenate([dw_weight, tile_embed, conv_bias[None, :]]))
    block_in, conv = depthwise(
        seq_index, first_crop, crop_counts, slots, before, after, table
    )
    cells = PER_DEV * side * side
    conv_t = conv.astype(jnp.float16)
    conv_all = lax.all_gather(conv_t, TP, axis=0, tiled=True).astype(f32)
    normed = layer_norm(conv_all, ln_gain, ln_bias)
    sums = mlp_sum(normed, blocks, b_up, width)
    result = pl.pallas_call(
        last_kernel,
        out_shape=jax.ShapeDtypeStruct((cells, width), jnp.bfloat16),
        in_specs=[whole()] * (len(sums) + 3),
        out_specs=whole(),
        compiler_params=vmem(12),
        name="result",
    )(*sums, b_down.astype(f32)[:, None], gamma[:, None], block_in)
    return result.reshape(PER_DEV, side, side, width)


def solution(mesh):
    fine = Mesh(mesh.devices.reshape(NY, NZ, NX, NCORE), SEQ + TP)
    placed = (
        P(SEQ, None, None, None), P(), P(), P(), P(), P(), P(), P(),
        P(SEQ, TP), P(TP), P(TP, SEQ), P(TP), P(TP),
    )
    return jax.shard_map(
        per_device,
        mesh=fine,
        in_specs=placed,
        out_specs=P(SEQ, None, None, TP),
        check_vma=False,
    )
```
